256 devices in a mesh: pop: 32 (over x, y, core), site: 8 (over z).
Axes of the slice: x: 4, y: 4, z: 8, core: 2. Of those that a mesh axis runs over, the one named last changes fastest.
Arguments:
- profile: bfloat16 [32768, 96], P(('pop', 'site')), may hold values from 0 to 1
- panel: bfloat16 [32768, 128], P(('pop', 'site')), may hold values from -6 to 6
- visit_person: int32 [131072], P(('pop', 'site')), may hold values from 0 to 127
- visit_owner: int32 [131072], P(('pop', 'site')), may hold values from 0 to 31, as said below
- visit_row: int32 [131072], P(('pop', 'site')), may hold values from 0 to 1023, as said below
- visit_start: int32 [131072], P(('pop', 'site')), may hold values from 0 to 95
- visit_length: int32 [131072], P(('pop', 'site')), may hold values from 2 to 48
- tile_loc: int32 [2048], P(('pop', 'site')), may hold values from 0 to 7
Outputs:
- exposure: bfloat16 [32768, 128], P(('pop', 'site'))
The draws below stay inside these ranges and needn't reach their ends.
Inputs may be any that keep to these rules, and one draw needn't show every extreme that they name: `visit_owner`: all devices with one site index send the same number of visits to a given owner index; at most 24 visits of one device go to one owner index, and in every draw some owner index receives exactly 24 from every device of a site index. `visit_row`: among the visits that reach one owner device the rows are distinct; in each tile the rows that are used come first and the rest are empty.
All inputs are finite; a program needn't handle non-finite values.
Results may differ from the reference program's by a relative error of at most 0.013.
Values may be sent and summed in bfloat16 or wider, within the bound.
No kernel may reach another device: no remote copies, remote signals or barrier semaphores. Data moves between devices by JAX's collectives and lax.ppermute only.
A program may use at most 64 MiB of HBM per device.

```python
import jax
import jax.numpy as jnp
from jax import lax

SLOTS = 96
PANEL = 128
VIS_DEV = 512
PER_DEV = 128
BASE = 16
TILES_DEV = 8
ROWS_DEV = 1024
LOC_GRP = 8
VISITS = 131072
PERSONS = 32768
TILE_ALL = 2048
N_POP = 32
N_SITE = 8


def plan_visits(key):
    base_key = jax.random.fold_in(key, 4242)
    key_perm, key_delta, key_fill, key_rank, key_order = jax.random.split(base_key, 5)
    perm_keys = jax.random.split(key_perm, N_SITE)
    owner_order = jax.vmap(lambda subkey: jax.random.permutation(subkey, N_POP))(perm_keys)
    half_pop = N_POP // 2
    deltas = jax.random.randint(key_delta, (N_SITE, half_pop), 0, BASE // 2 + 1)
    deltas = deltas.at[:, 0].set(BASE // 2)
    by_place = jnp.stack([BASE + deltas, BASE - deltas], axis=-1).reshape(N_SITE, N_POP)
    site_ids = jnp.broadcast_to(jnp.arange(N_SITE, dtype=jnp.int32)[:, None], (N_SITE, N_POP))
    counts = jnp.zeros((N_SITE, N_POP), jnp.int32).at[site_ids, owner_order].set(by_place)
    live_total = N_POP * counts
    tile_ids = jnp.arange(TILES_DEV, dtype=jnp.int32)
    spread = live_total[..., None] * (tile_ids + 1) // TILES_DEV - live_total[..., None] * tile_ids // TILES_DEV
    shakes = jax.random.randint(key_fill, (N_SITE, N_POP, TILES_DEV // 2), 0, 17)
    filled = spread + jnp.stack([shakes, -shakes], axis=-1).reshape(N_SITE, N_POP, TILES_DEV)
    row_ids = jnp.arange(ROWS_DEV, dtype=jnp.int32)
    is_live = (row_ids % 128)[None, None, :] < jnp.repeat(filled, 128, axis=-1)
    scores = jnp.where(is_live, jax.random.randint(key_rank, (N_SITE, N_POP, ROWS_DEV), 0, ROWS_DEV), ROWS_DEV + row_ids)
    ordering = jnp.argsort(scores, axis=-1, stable=True)
    ranking = jnp.argsort(ordering, axis=-1, stable=True)
    sender_pop = ranking // jnp.maximum(counts, 1)[..., None]
    sender_dev = sender_pop * N_SITE + site_ids[..., None]
    spacing = 4096
    sort_keys = jnp.where(is_live, sender_dev * spacing + jax.random.randint(key_order, (N_SITE, N_POP, ROWS_DEV), 0, spacing), N_POP * N_SITE * spacing)
    picked = jnp.argsort(sort_keys.reshape(-1), stable=True)[:VISITS]
    owners = (picked // ROWS_DEV % N_POP).astype(jnp.int32)
    buffer_rows = (picked % ROWS_DEV).astype(jnp.int32)
    return (owners, buffer_rows)


def draw_visit_owner(key, part):
    return plan_visits(key)[0]


def draw_visit_row(key, part):
    return plan_visits(key)[1]


def with_ends(entries, rng, low, top_value):
    longest = entries.shape.index(max(entries.shape))
    spots = []
    for shift in (0, 1):
        where = [jax.random.randint(jax.random.fold_in(rng, axis), (), 0, length) for axis, length in enumerate(entries.shape)]
        where[longest] = (where[longest] + shift) % entries.shape[longest]
        spots.append(tuple(where))
    return entries.at[spots[0]].set(low).at[spots[1]].set(top_value)


def level_of(key, dims, cuts, least, top_value):
    factor_of, own = 1.0, jax.random.fold_in(key, 6)
    for position, shards_of in cuts:
        heights = jnp.exp(jax.random.uniform(jax.random.fold_in(own, position), (shards_of,), jnp.float32, least / len(cuts), top_value / len(cuts)))
        factor_of = factor_of * jnp.repeat(heights, dims[position] // shards_of).reshape([-1 if axis == position else 1 for axis in range(len(dims))])
    return factor_of


def gaussian(own_key, dims, scale, limit, cuts=(), kind=jnp.bfloat16):
    array = jax.random.normal(own_key, dims, jnp.float32) * scale
    if len(cuts) > 0:
        array = level_of(own_key, dims, cuts, -0.22, 0.18) * array
    return jnp.clip(array, min=-limit, max=limit).astype(kind)


def setup_inputs(seed: int = 0) -> dict:
    key_of = jax.random.split(jax.random.key(seed), 9)
    return {
        "profile": jnp.clip(1.0 * jax.random.uniform(key_of[0], (PERSONS, SLOTS), jnp.float32) ** level_of(key_of[0], (PERSONS, SLOTS), ((0, 256),), -0.2, 0.2), 0.0, 1.0).astype(jnp.bfloat16),
        "panel": gaussian(key_of[1], (PERSONS, PANEL), 1.0, 6.0, ((0, 256),)),
        "visit_person": with_ends(jax.random.randint(key_of[2], (VISITS,), 0, PER_DEV), jax.random.fold_in(key_of[2], 1), 0, PER_DEV - 1).astype(jnp.int32),
        "visit_owner": draw_visit_owner(jax.random.fold_in(key_of[8], 71), 0),
        "visit_row": draw_visit_row(jax.random.fold_in(key_of[8], 71), 0),
        "visit_start": with_ends(jax.random.randint(key_of[5], (VISITS,), 0, SLOTS), jax.random.fold_in(key_of[5], 1), 0, SLOTS - 1).astype(jnp.int32),
        "visit_length": with_ends(jax.random.randint(key_of[6], (VISITS,), 2, SLOTS // 2 + 1), jax.random.fold_in(key_of[6], 1), 2, (SLOTS // 2 + 1) - 1).astype(jnp.int32),
        "tile_loc": with_ends(jax.random.randint(key_of[7], (TILE_ALL,), 0, LOC_GRP), jax.random.fold_in(key_of[7], 1), 0, LOC_GRP - 1).astype(jnp.int32),
    }


def reference(profile, panel, visit_person, visit_owner, visit_row, visit_start, visit_length, tile_loc):
    device_total = N_POP * N_SITE
    visit_ids = jnp.arange(VISITS, dtype=jnp.int32)
    sender = visit_ids // VIS_DEV
    person = (sender * PER_DEV + visit_person).astype(jnp.int32)
    slot_ids = jnp.arange(SLOTS, dtype=jnp.int32)
    finish = jnp.minimum(visit_start + visit_length, SLOTS)
    inside = (slot_ids[None, :] >= visit_start[:, None]) & (slot_ids[None, :] < finish[:, None])
    weights = jnp.where(inside, profile[person], jnp.zeros((), profile.dtype))
    visit_panel = panel[person]
    owner_dev = visit_owner * N_SITE + sender % N_SITE
    target = (owner_dev * ROWS_DEV + visit_row).astype(jnp.int32)
    buf_weights = jnp.zeros((device_total * ROWS_DEV, SLOTS), profile.dtype).at[target].set(weights)
    buf_panel = jnp.zeros((device_total * ROWS_DEV, PANEL), panel.dtype).at[target].set(visit_panel)
    shaped_w = buf_weights.reshape(N_POP, N_SITE, TILES_DEV, 128, SLOTS).astype(jnp.float32)
    shaped_p = buf_panel.reshape(N_POP, N_SITE, TILES_DEV, 128, PANEL).astype(jnp.float32)
    highest = lax.Precision.HIGHEST
    moments = jnp.einsum("gxtrs,gxtrc->gxtsc", shaped_w, shaped_p, precision=highest)
    place_ids = jnp.arange(LOC_GRP, dtype=jnp.int32)
    place_hot = (tile_loc.reshape(N_POP, N_SITE, TILES_DEV)[..., None] == place_ids).astype(jnp.float32)
    loc_moment = jnp.einsum("gxtl,gxtsc->glsc", place_hot, moments, precision=highest)
    tile_moments = jnp.einsum("gxtl,glsc->gxtsc", place_hot, loc_moment, precision=highest)
    summed = jnp.einsum("gxtrs,gxtsc->gxtrc", shaped_w, tile_moments, precision=highest)
    row_result = (summed / SLOTS).astype(jnp.bfloat16).reshape(device_total * ROWS_DEV, PANEL)
    visit_result = row_result[target]
    exposure = jax.ops.segment_sum(visit_result.astype(jnp.float32), person, num_segments=PERSONS)
    return exposure.astype(jnp.bfloat16)
```

```python
import jax
import jax.numpy as jnp
from jax import lax
from jax.experimental import pallas as pl
from jax.experimental.pallas import tpu as pltpu
from jax.sharding import PartitionSpec as P

BF16 = jnp.bfloat16
F32 = jnp.float32
LOCATIONS = 8
NT = (((1,), (1,)), ((), ()))


def iota(shape, axis):
    return lax.broadcasted_iota(jnp.int32, shape, axis)


def matmul(a, b):
    return jnp.dot(a, b, preferred_element_type=F32)


def matmul_nt(a, b):
    return lax.dot_general(a, b, NT, preferred_element_type=F32)


def as_bf16(mask):
    return jnp.where(mask, 1.0, 0.0).astype(BF16)


def pack_kernel(
    pop_count,
    profile_ref,
    panel_ref,
    person_ref,
    owner_ref,
    row_ref,
    start_ref,
    length_ref,
    send_ref,
    persons_ref,
    wide_ref,
):
    visits = person_ref.shape[1]
    persons, slots = profile_ref.shape
    rows = send_ref.shape[0]
    capacity = rows // pop_count
    owner = owner_ref[...]
    start = start_ref[...]
    finish = jnp.minimum(start + length_ref[...], slots)
    tile = row_ref[...] >> 7
    owner_hot = iota((pop_count, visits), 0) == owner
    earlier = as_bf16(iota((visits, visits), 0) < iota((visits, visits), 1))
    before = matmul(as_bf16(owner_hot), earlier)
    position = jnp.sum(jnp.where(owner_hot, before, 0.0), axis=0, keepdims=True)
    slot = owner * capacity + position.astype(jnp.int32)
    place = as_bf16(iota((rows, visits), 0) == slot)
    person_hot = as_bf16(iota((persons, visits), 0) == person_ref[...])
    line = iota((128, visits), 0)
    facts = jnp.where(line == 0, start, jnp.where(line == 1, finish, jnp.where(line == 2, tile, 0)))
    table = jnp.concatenate([person_hot, facts.astype(F32).astype(BF16)], axis=0)
    placed = matmul_nt(place, table)
    hot = placed[:, :persons].astype(BF16)
    start_at = placed[:, persons : persons + 1]
    finish_at = placed[:, persons + 1 : persons + 2]
    tile_at = placed[:, persons + 2 : persons + 3]
    wide_ref[...] = jnp.zeros_like(wide_ref)
    wide_ref[:, :slots] = profile_ref[...]
    weights = matmul(hot, wide_ref[...])
    lane = iota((rows, 128), 1)
    lane_f = lane.astype(F32)
    inside = (lane_f >= start_at) & (lane_f < finish_at)
    weights = jnp.where(inside, weights, 0.0)
    weights = jnp.where(lane == slots, tile_at, weights)
    send_ref[:, :128] = weights.astype(BF16)
    send_ref[:, 128:] = matmul(hot, panel_ref[...]).astype(BF16)
    persons_ref[...] = matmul_nt(person_hot, place).astype(BF16)


def moment_kernel(slots, tile_loc_ref, got_ref, moment_ref):
    rows = got_ref.shape[0]
    unit = as_bf16(iota((128, 128), 0) == iota((128, 128), 1))
    flipped = matmul_nt(unit, got_ref[:, :128])
    tile = flipped[slots : slots + 1, :].astype(jnp.int32)
    place = jnp.zeros((1, rows), jnp.int32)
    for t in range(tile_loc_ref.shape[0]):
        place = jnp.where(tile == t, tile_loc_ref[t], place)
    weights = flipped[:slots, :]
    masked = [jnp.where(place == l, weights, 0.0).astype(BF16) for l in range(LOCATIONS)]
    moment = matmul(jnp.concatenate(masked, axis=0), got_ref[:, 128:])
    moment_ref[...] = moment.reshape(moment_ref.shape).astype(moment_ref.dtype)


def apply_kernel(slots, tile_loc_ref, got_ref, total_ref, result_ref, high_ref, low_ref):
    rows = got_ref.shape[0]
    tile = got_ref[:, slots : slots + 1].astype(F32).astype(jnp.int32)
    place = jnp.zeros((rows, 1), jnp.int32)
    for t in range(tile_loc_ref.shape[0]):
        place = jnp.where(tile == t, tile_loc_ref[t], place)
    high_ref[...] = jnp.zeros_like(high_ref)
    low_ref[...] = jnp.zeros_like(low_ref)
    for l in range(LOCATIONS):
        total = total_ref[l].astype(F32)
        high = total.astype(BF16)
        high_ref[pl.ds(l * 128, slots), :] = high
        low_ref[pl.ds(l * 128, slots), :] = (total - high.astype(F32)).astype(BF16)
    weights = got_ref[:, :128].astype(F32)
    weights = jnp.where(iota((rows, 128), 1) < slots, weights, 0.0)
    spread = jnp.concatenate(
        [jnp.where(place == l, weights, 0.0).astype(BF16) for l in range(LOCATIONS)], axis=1
    )
    result = matmul(spread, high_ref[...]) + matmul(spread, low_ref[...])
    result_ref[...] = (result / slots).astype(BF16)


def finish_kernel(persons_ref, results_ref, out_ref):
    out_ref[...] = matmul(persons_ref[...], results_ref[...]).astype(BF16)


def vmem(count):
    return [pl.BlockSpec(memory_space=pltpu.VMEM)] * count


def per_device(
    profile, panel, visit_person, visit_owner, visit_row, visit_start, visit_length, tile_loc
):
    pop_count = lax.axis_size("pop")
    visits = visit_person.shape[0]
    persons, slots = profile.shape
    width = panel.shape[1]
    capacity = visits // pop_count * 3 // 2
    rows = pop_count * capacity
    as_row = lambda x: x.reshape(1, visits)
    send, person_rows = pl.pallas_call(
        lambda *refs: pack_kernel(pop_count, *refs),
        out_shape=(
            jax.ShapeDtypeStruct((rows, 128 + width), BF16),
            jax.ShapeDtypeStruct((persons, rows), BF16),
        ),
        in_specs=vmem(7),
        out_specs=tuple(vmem(2)),
        scratch_shapes=[pltpu.VMEM((persons, 128), BF16)],
        name="pack",
    )(
        profile,
        panel,
        as_row(visit_person),
        as_row(visit_owner),
        as_row(visit_row),
        as_row(visit_start),
        as_row(visit_length),
    )
    got = lax.all_to_all(
        send.reshape(pop_count, capacity, 128 + width), "pop", 0, 0, tiled=True
    ).reshape(rows, 128 + width)
    smem = pl.BlockSpec(memory_space=pltpu.SMEM)
    moment = pl.pallas_call(
        lambda *refs: moment_kernel(slots, *refs),
        out_shape=jax.ShapeDtypeStruct((LOCATIONS, slots, width), F32),
        in_specs=[smem] + vmem(1),
        out_specs=vmem(1)[0],
        name="moments",
    )(tile_loc, got)
    total = lax.psum(moment, "site")
    result = pl.pallas_call(
        lambda *refs: apply_kernel(slots, *refs),
        out_shape=jax.ShapeDtypeStruct((rows, width), BF16),
        in_specs=[smem] + vmem(2),
        out_specs=vmem(1)[0],
        scratch_shapes=[pltpu.VMEM((LOCATIONS * 128, width), BF16)] * 2,
        name="apply",
    )(tile_loc, got, total)
    returned = lax.all_to_all(
        result.reshape(pop_count, capacity, width), "pop", 0, 0, tiled=True
    ).reshape(rows, width)
    return pl.pallas_call(
        finish_kernel,
        out_shape=jax.ShapeDtypeStruct((persons, width), BF16),
        in_specs=vmem(2),
        out_specs=vmem(1)[0],
        name="finish",
    )(person_rows, returned)


def solution(mesh):
    both = P(("pop", "site"))
    wide = P(("pop", "site"), None)
    return jax.shard_map(
        per_device,
        mesh=mesh,
        in_specs=(wide, wide, both, both, both, both, both, both),
        out_specs=wide,
        check_vma=False,
    )
```

```python
import jax
import jax.numpy as jnp
from jax import lax
from jax.experimental import pallas as pl
from jax.experimental.pallas import tpu as pltpu
from jax.sharding import PartitionSpec as P

BF16 = jnp.bfloat16
F32 = jnp.float32
LOCATIONS = 8
NT = (((1,), (1,)), ((), ()))


def iota(shape, axis):
    return lax.broadcasted_iota(jnp.int32, shape, axis)


def matmul(a, b):
    return jnp.dot(a, b, preferred_element_type=F32)


def matmul_nt(a, b):
    return lax.dot_general(a, b, NT, preferred_element_type=F32)


def as_bf16(mask):
    return jnp.where(mask, 1.0, 0.0).astype(BF16)


def pack_kernel(
    pop_count,
    profile_ref,
    panel_ref,
    person_ref,
    owner_ref,
    row_ref,
    start_ref,
    length_ref,
    send_ref,
    persons_ref,
):
    visits = person_ref.shape[1]
    slots, persons = profile_ref.shape
    rows = send_ref.shape[0]
    capacity = rows // pop_count
    owner = owner_ref[...]
    start = start_ref[...]
    finish = jnp.minimum(start + length_ref[...], slots)
    tile = row_ref[...] >> 7
    owner_hot = iota((pop_count, visits), 0) == owner
    earlier = as_bf16(iota((visits, visits), 0) < iota((visits, visits), 1))
    before = matmul(as_bf16(owner_hot), earlier)
    position = jnp.sum(jnp.where(owner_hot, before, 0.0), axis=0, keepdims=True)
    slot = owner * capacity + position.astype(jnp.int32)
    place = as_bf16(iota((rows, visits), 0) == slot)
    person_hot = as_bf16(iota((persons, visits), 0) == person_ref[...])
    line = iota((128, visits), 0)
    facts = jnp.where(line == 0, start, jnp.where(line == 1, finish, jnp.where(line == 2, tile, 0)))
    table = jnp.concatenate([person_hot, facts.astype(F32).astype(BF16)], axis=0)
    placed = matmul_nt(place, table)
    hot = placed[:, :persons].astype(BF16)
    start_at = placed[:, persons : persons + 1]
    finish_at = placed[:, persons + 1 : persons + 2]
    tile_at = placed[:, persons + 2 : persons + 3]
    no_slots = jnp.zeros((128 - slots, persons), BF16)
    weights = matmul_nt(hot, jnp.concatenate([profile_ref[...], no_slots], axis=0))
    lane = iota((rows, 128), 1)
    lane_f = lane.astype(F32)
    inside = (lane_f >= start_at) & (lane_f < finish_at)
    weights = jnp.where(inside, weights, 0.0)
    weights = jnp.where(lane == slots, tile_at, weights)
    send_ref[:, :128] = weights.astype(BF16)
    send_ref[:, 128:] = matmul(hot, panel_ref[...]).astype(BF16)
    persons_ref[...] = matmul_nt(person_hot, place).astype(BF16)


def moment_kernel(slots, tile_loc_ref, got_ref, moment_ref):
    rows = got_ref.shape[0]
    unit = as_bf16(iota((128, 128), 0) == iota((128, 128), 1))
    flipped = matmul_nt(unit, got_ref[:, :128])
    tile = flipped[slots : slots + 1, :].astype(jnp.int32)
    place = jnp.zeros((1, rows), jnp.int32)
    for t in range(tile_loc_ref.shape[0]):
        place = jnp.where(tile == t, tile_loc_ref[t], place)
    weights = flipped[:slots, :]
    masked = [jnp.where(place == l, weights, 0.0).astype(BF16) for l in range(LOCATIONS)]
    moment = matmul(jnp.concatenate(masked, axis=0), got_ref[:, 128:])
    moment_ref[...] = moment.reshape(moment_ref.shape).astype(moment_ref.dtype)


def sum_kernel(parts_ref, copies_ref):
    total = jnp.sum(parts_ref[...].astype(F32), axis=0).astype(BF16)
    for member in range(copies_ref.shape[0]):
        copies_ref[member] = total


def apply_kernel(slots, tile_loc_ref, got_ref, total_ref, result_ref, wide_ref):
    rows = got_ref.shape[0]
    tile = got_ref[:, slots : slots + 1].astype(F32).astype(jnp.int32)
    place = jnp.zeros((rows, 1), jnp.int32)
    for t in range(tile_loc_ref.shape[0]):
        place = jnp.where(tile == t, tile_loc_ref[t], place)
    for l in range(LOCATIONS):
        wide_ref[pl.ds(l * 128, slots), :] = total_ref[l]
        wide_ref[pl.ds(l * 128 + slots, 128 - slots), :] = jnp.zeros((128 - slots, 128), BF16)
    weights = got_ref[:, :128].astype(F32)
    weights = jnp.where(iota((rows, 128), 1) < slots, weights, 0.0)
    spread = jnp.concatenate(
        [jnp.where(place == l, weights, 0.0).astype(BF16) for l in range(LOCATIONS)], axis=1
    )
    result = matmul(spread, wide_ref[...])
    result_ref[...] = (result / slots).astype(BF16)


def finish_kernel(persons_ref, results_ref, out_ref):
    out_ref[...] = matmul(persons_ref[...], results_ref[...]).astype(BF16)


def vmem(count):
    return [pl.BlockSpec(memory_space=pltpu.VMEM)] * count


def per_device(
    profile, panel, visit_person, visit_owner, visit_row, visit_start, visit_length, tile_loc
):
    pop_count = lax.axis_size("pop")
    visits = visit_person.shape[0]
    persons, slots = profile.shape
    width = panel.shape[1]
    capacity = visits // pop_count * 3 // 2
    rows = pop_count * capacity
    as_row = lambda x: x.reshape(1, visits)
    send, person_rows = pl.pallas_call(
        lambda *refs: pack_kernel(pop_count, *refs),
        out_shape=(
            jax.ShapeDtypeStruct((rows, 128 + width), BF16),
            jax.ShapeDtypeStruct((persons, rows), BF16),
        ),
        in_specs=vmem(7),
        out_specs=tuple(vmem(2)),
        name="pack",
    )(
        profile.T,
        panel,
        as_row(visit_person),
        as_row(visit_owner),
        as_row(visit_row),
        as_row(visit_start),
        as_row(visit_length),
    )
    got = lax.all_to_all(
        send.reshape(pop_count, capacity, 128 + width), "pop", 0, 0, tiled=True
    ).reshape(rows, 128 + width)
    smem = pl.BlockSpec(memory_space=pltpu.SMEM)
    moment = pl.pallas_call(
        lambda *refs: moment_kernel(slots, *refs),
        out_shape=jax.ShapeDtypeStruct((LOCATIONS, slots, width), BF16),
        in_specs=[smem] + vmem(1),
        out_specs=vmem(1)[0],
        name="moments",
    )(tile_loc, got)
    parts = lax.all_to_all(moment, "site", 0, 0, tiled=True)
    copies = pl.pallas_call(
        sum_kernel,
        out_shape=jax.ShapeDtypeStruct((LOCATIONS, slots, width), BF16),
        in_specs=vmem(1),
        out_specs=vmem(1)[0],
        name="sum_parts",
    )(parts)
    total = lax.all_to_all(copies, "site", 0, 0, tiled=True)
    result = pl.pallas_call(
        lambda *refs: apply_kernel(slots, *refs),
        out_shape=jax.ShapeDtypeStruct((rows, width), BF16),
        in_specs=[smem] + vmem(2),
        out_specs=vmem(1)[0],
        scratch_shapes=[pltpu.VMEM((LOCATIONS * 128, width), BF16)],
        name="apply",
    )(tile_loc, got, total)
    returned = lax.all_to_all(
        result.reshape(pop_count, capacity, width), "pop", 0, 0, tiled=True
    ).reshape(rows, width)
    return pl.pallas_call(
        finish_kernel,
        out_shape=jax.ShapeDtypeStruct((persons, width), BF16),
        in_specs=vmem(2),
        out_specs=vmem(1)[0],
        name="finish",
    )(person_rows, returned)


def solution(mesh):
    both = P(("pop", "site"))
    wide = P(("pop", "site"), None)
    return jax.shard_map(
        per_device,
        mesh=mesh,
        in_specs=(wide, wide, both, both, both, both, both, both),
        out_specs=wide,
        check_vma=False,
    )
```

```python
import jax
import jax.numpy as jnp
from jax import lax
from jax.experimental import pallas as pl
from jax.experimental.pallas import tpu as pltpu
from jax.sharding import PartitionSpec as P

BF16 = jnp.bfloat16
F32 = jnp.float32
LOCATIONS = 8
NT = (((1,), (1,)), ((), ()))


def iota(shape, axis):
    return lax.broadcasted_iota(jnp.int32, shape, axis)


def matmul(a, b):
    return jnp.dot(a, b, preferred_element_type=F32)


def matmul_nt(a, b):
    return lax.dot_general(a, b, NT, preferred_element_type=F32)


def as_bf16(mask):
    return jnp.where(mask, 1.0, 0.0).astype(BF16)


def pack_kernel(
    pop_count,
    profile_ref,
    panel_ref,
    person_ref,
    owner_ref,
    row_ref,
    start_ref,
    length_ref,
    send_ref,
    persons_ref,
):
    visits = person_ref.shape[1]
    slots, persons = profile_ref.shape
    rows = send_ref.shape[0]
    capacity = rows // pop_count
    owner = owner_ref[...]
    start = start_ref[...]
    finish = jnp.minimum(start + length_ref[...], slots)
    tile = row_ref[...] >> 7
    owner_hot = iota((pop_count, visits), 0) == owner
    earlier = as_bf16(iota((visits, visits), 0) < iota((visits, visits), 1))
    before = matmul(as_bf16(owner_hot), earlier)
    position = jnp.sum(jnp.where(owner_hot, before, 0.0), axis=0, keepdims=True)
    slot = owner * capacity + position.astype(jnp.int32)
    place = as_bf16(iota((rows, visits), 0) == slot)
    person_hot = as_bf16(iota((persons, visits), 0) == person_ref[...])
    line = iota((128, visits), 0)
    facts = jnp.where(line == 0, start, jnp.where(line == 1, finish, jnp.where(line == 2, tile, 0)))
    table = jnp.concatenate([person_hot, facts.astype(F32).astype(BF16)], axis=0)
    placed = matmul_nt(place, table)
    hot = placed[:, :persons].astype(BF16)
    start_at = placed[:, persons : persons + 1]
    finish_at = placed[:, persons + 1 : persons + 2]
    tile_at = placed[:, persons + 2 : persons + 3]
    no_slots = jnp.zeros((128 - slots, persons), BF16)
    weights = matmul_nt(hot, jnp.concatenate([profile_ref[...], no_slots], axis=0))
    lane = iota((rows, 128), 1)
    lane_f = lane.astype(F32)
    inside = (lane_f >= start_at) & (lane_f < finish_at)
    weights = jnp.where(inside, weights, 0.0)
    weights = jnp.where(lane == slots, tile_at, weights)
    send_ref[:, :128] = weights.astype(BF16)
    send_ref[:, 128:] = matmul(hot, panel_ref[...]).astype(BF16)
    persons_ref[...] = matmul_nt(person_hot, place).astype(BF16)


def moment_kernel(slots, tile_loc_ref, got_ref, moment_ref):
    rows = got_ref.shape[0]
    unit = as_bf16(iota((128, 128), 0) == iota((128, 128), 1))
    flipped = matmul_nt(unit, got_ref[:, :128])
    tile = flipped[slots : slots + 1, :].astype(jnp.int32)
    place = jnp.zeros((1, rows), jnp.int32)
    for t in range(tile_loc_ref.shape[0]):
        place = jnp.where(tile == t, tile_loc_ref[t], place)
    weights = flipped[:slots, :]
    masked = [jnp.where(place == l, weights, 0.0).astype(BF16) for l in range(LOCATIONS)]
    moment = matmul(jnp.concatenate(masked, axis=0), got_ref[:, 128:])
    moment_ref[...] = moment.reshape(moment_ref.shape).astype(moment_ref.dtype)


def sum_kernel(parts_ref, copies_ref):
    total = jnp.sum(parts_ref[...].astype(F32), axis=0).astype(BF16)
    for member in range(copies_ref.shape[0]):
        copies_ref[member] = total


def apply_kernel(slots, tile_loc_ref, got_ref, total_ref, result_ref, wide_ref):
    rows = got_ref.shape[0]
    tile = got_ref[:, slots : slots + 1].astype(F32).astype(jnp.int32)
    place = jnp.zeros((rows, 1), jnp.int32)
    for t in range(tile_loc_ref.shape[0]):
        place = jnp.where(tile == t, tile_loc_ref[t], place)
    for l in range(LOCATIONS):
        wide_ref[pl.ds(l * 128, slots), :] = total_ref[l]
        wide_ref[pl.ds(l * 128 + slots, 128 - slots), :] = jnp.zeros((128 - slots, 128), BF16)
    weights = got_ref[:, :128].astype(F32)
    weights = jnp.where(iota((rows, 128), 1) < slots, weights, 0.0)
    spread = jnp.concatenate(
        [jnp.where(place == l, weights, 0.0).astype(BF16) for l in range(LOCATIONS)], axis=1
    )
    result = matmul(spread, wide_ref[...])
    result_ref[...] = (result / slots).astype(BF16)


def finish_kernel(persons_ref, results_ref, out_ref):
    out_ref[...] = matmul(persons_ref[...], results_ref[...]).astype(BF16)


def vmem(count):
    return [pl.BlockSpec(memory_space=pltpu.VMEM)] * count


def exchange(array, axis):
    blocks = array.reshape((lax.axis_size(axis), -1, array.shape[-1]))
    moved = lax.all_to_all(blocks, axis, 0, 0, tiled=True).reshape(array.shape)
    return pltpu.with_memory_space_constraint(moved, pltpu.VMEM)


def per_device(
    profile, panel, visit_person, visit_owner, visit_row, visit_start, visit_length, tile_loc
):
    pop_count = lax.axis_size("pop")
    visits = visit_person.shape[0]
    persons, slots = profile.shape
    width = panel.shape[1]
    capacity = visits // pop_count * 3 // 2
    rows = pop_count * capacity
    as_row = lambda x: x.reshape(1, visits)
    send, person_rows = pl.pallas_call(
        lambda *refs: pack_kernel(pop_count, *refs),
        out_shape=(
            pltpu.VMEM((rows, 128 + width), BF16),
            pltpu.VMEM((persons, rows), BF16),
        ),
        in_specs=vmem(7),
        out_specs=tuple(vmem(2)),
        name="pack",
    )(
        profile.T,
        panel,
        as_row(visit_person),
        as_row(visit_owner),
        as_row(visit_row),
        as_row(visit_start),
        as_row(visit_length),
    )
    got = exchange(send, "pop")
    smem = pl.BlockSpec(memory_space=pltpu.SMEM)
    moment = pl.pallas_call(
        lambda *refs: moment_kernel(slots, *refs),
        out_shape=pltpu.VMEM((LOCATIONS, slots, width), BF16),
        in_specs=[smem] + vmem(1),
        out_specs=vmem(1)[0],
        name="moments",
    )(tile_loc, got)
    parts = exchange(moment, "site")
    copies = pl.pallas_call(
        sum_kernel,
        out_shape=pltpu.VMEM((LOCATIONS, slots, width), BF16),
        in_specs=vmem(1),
        out_specs=vmem(1)[0],
        name="sum_parts",
    )(parts)
    total = exchange(copies, "site")
    result = pl.pallas_call(
        lambda *refs: apply_kernel(slots, *refs),
        out_shape=pltpu.VMEM((rows, width), BF16),
        in_specs=[smem] + vmem(2),
        out_specs=vmem(1)[0],
        scratch_shapes=[pltpu.VMEM((LOCATIONS * 128, width), BF16)],
        name="apply",
    )(tile_loc, got, total)
    returned = exchange(result, "pop")
    return pl.pallas_call(
        finish_kernel,
        out_shape=jax.ShapeDtypeStruct((persons, width), BF16),
        in_specs=vmem(2),
        out_specs=vmem(1)[0],
        name="finish",
    )(pltpu.with_memory_space_constraint(person_rows, pltpu.VMEM), returned)


def solution(mesh):
    both = P(("pop", "site"))
    wide = P(("pop", "site"), None)
    return jax.shard_map(
        per_device,
        mesh=mesh,
        in_specs=(wide, wide, both, both, both, both, both, both),
        out_specs=wide,
        check_vma=False,
    )
```

```python
import jax
import jax.numpy as jnp
from jax import lax
from jax.experimental import pallas as pl
from jax.experimental.pallas import tpu as pltpu
from jax.sharding import PartitionSpec as P

BF16 = jnp.bfloat16
F32 = jnp.float32
LOCATIONS = 8
HALF = LOCATIONS // 2
TILES = 8
NT = (((1,), (1,)), ((), ()))


def iota(shape, axis):
    return lax.broadcasted_iota(jnp.int32, shape, axis)


def matmul(a, b):
    return jnp.dot(a, b, preferred_element_type=F32)


def matmul_nt(a, b):
    return lax.dot_general(a, b, NT, preferred_element_type=F32)


def as_bf16(mask):
    return jnp.where(mask, 1.0, 0.0).astype(BF16)


def pack_kernel(
    pop_count,
    profile_ref,
    panel_ref,
    person_ref,
    owner_ref,
    row_ref,
    start_ref,
    length_ref,
    send_ref,
    persons_ref,
):
    visits = person_ref.shape[1]
    slots, persons = profile_ref.shape
    rows = send_ref.shape[0]
    capacity = rows // pop_count
    owner = owner_ref[...]
    start = start_ref[...]
    finish = jnp.minimum(start + length_ref[...], slots)
    tile = (row_ref[...] >> 7) + TILES * (lax.axis_index("site") & 1)
    owner_hot = iota((pop_count, visits), 0) == owner
    earlier = as_bf16(iota((visits, visits), 0) < iota((visits, visits), 1))
    before = matmul(as_bf16(owner_hot), earlier)
    position = jnp.sum(jnp.where(owner_hot, before, 0.0), axis=0, keepdims=True)
    slot = owner * capacity + position.astype(jnp.int32)
    place = as_bf16(iota((rows, visits), 0) == slot)
    person_hot = as_bf16(iota((persons, visits), 0) == person_ref[...])
    line = iota((128, visits), 0)
    facts = jnp.where(line == 0, start, jnp.where(line == 1, finish, jnp.where(line == 2, tile, 0)))
    table = jnp.concatenate([person_hot, facts.astype(F32).astype(BF16)], axis=0)
    placed = matmul_nt(place, table)
    hot = placed[:, :persons].astype(BF16)
    start_at = placed[:, persons : persons + 1]
    finish_at = placed[:, persons + 1 : persons + 2]
    tile_at = placed[:, persons + 2 : persons + 3]
    no_slots = jnp.zeros((128 - slots, persons), BF16)
    weights = matmul_nt(hot, jnp.concatenate([profile_ref[...], no_slots], axis=0))
    lane = iota((rows, 128), 1)
    lane_f = lane.astype(F32)
    inside = (lane_f >= start_at) & (lane_f < finish_at)
    weights = jnp.where(inside, weights, 0.0)
    weights = jnp.where(lane == slots, tile_at, weights)
    send_ref[:, :128] = weights.astype(BF16)
    send_ref[:, 128:] = matmul(hot, panel_ref[...]).astype(BF16)
    persons_ref[...] = matmul_nt(person_hot, place).astype(BF16)


def place_of(tile, loc_refs):
    mine, sibling, neighbour, diagonal = loc_refs
    core = lax.axis_index("pop") & 1
    parity = lax.axis_index("site") & 1
    place = jnp.zeros(tile.shape, jnp.int32)
    for t in range(TILES):
        same = jnp.where(core == parity, mine[t], sibling[t])
        other = jnp.where(core == parity, neighbour[t], diagonal[t])
        place = jnp.where(tile == t, jnp.where(parity == 0, same, other), place)
        place = jnp.where(tile == TILES + t, jnp.where(parity == 0, other, same), place)
    return place ^ (HALF * core)


def moment_kernel(slots, *refs):
    loc_refs = refs[:4]
    got_ref, keep_ref, give_ref = refs[4:]
    unit = as_bf16(iota((128, 128), 0) == iota((128, 128), 1))
    flipped = matmul_nt(unit, got_ref[:, :128])
    place = place_of(flipped[slots : slots + 1, :].astype(jnp.int32), loc_refs)
    weights = flipped[:slots, :]
    masked = [jnp.where(place == l, weights, 0.0).astype(BF16) for l in range(LOCATIONS)]
    moment = matmul(jnp.concatenate(masked, axis=0), got_ref[:, 128:])
    keep_ref[...] = moment[: HALF * slots]
    give_ref[...] = moment[HALF * slots :].astype(BF16)


def add_kernel(own_ref, far_ref, sum_ref, give_ref):
    total = own_ref[...] + far_ref[...].astype(F32)
    sum_ref[...] = total
    give_ref[...] = total.astype(BF16)


def last_add_kernel(own_ref, far_ref, give_ref):
    give_ref[...] = (own_ref[...] + far_ref[...].astype(F32)).astype(BF16)


def apply_kernel(slots, *refs):
    loc_refs = refs[:4]
    got_ref, own_ref, other_ref, result_ref, wide_ref = refs[4:]
    rows = got_ref.shape[0]
    place = place_of(got_ref[:, slots : slots + 1].astype(F32).astype(jnp.int32), loc_refs)
    for l in range(LOCATIONS):
        half_ref = own_ref if l < HALF else other_ref
        wide_ref[pl.ds(l * 128, slots), :] = half_ref[pl.ds(l % HALF * slots, slots), :]
        wide_ref[pl.ds(l * 128 + slots, 128 - slots), :] = jnp.zeros((128 - slots, 128), BF16)
    weights = got_ref[:, :128].astype(F32)
    weights = jnp.where(iota((rows, 128), 1) < slots, weights, 0.0)
    spread = jnp.concatenate(
        [jnp.where(place == l, weights, 0.0).astype(BF16) for l in range(LOCATIONS)], axis=1
    )
    result = matmul(spread, wide_ref[...])
    result_ref[...] = (result / slots).astype(BF16)


def finish_kernel(persons_ref, results_ref, out_ref):
    out_ref[...] = matmul(persons_ref[...], results_ref[...]).astype(BF16)


def vmem(count):
    return [pl.BlockSpec(memory_space=pltpu.VMEM)] * count


def in_vmem(array):
    return pltpu.with_memory_space_constraint(array, pltpu.VMEM)


def exchange(array):
    pops, sites = lax.axis_size("pop"), lax.axis_size("site")
    groups = [
        [(pop * 2 + core) * sites + pair * 2 + odd for pop in range(pops // 2) for odd in range(2)]
        for core in range(2)
        for pair in range(sites // 2)
    ]
    blocks = array.reshape((pops, -1, array.shape[-1]))
    moved = lax.all_to_all(
        blocks, ("pop", "site"), 0, 0, tiled=True, axis_index_groups=groups
    )
    return in_vmem(moved.reshape(array.shape))


def swap(array, pop_partner, site_partner):
    pops, sites = lax.axis_size("pop"), lax.axis_size("site")
    pairs = [
        (pop * sites + site, pop_partner(pop) * sites + site_partner(site))
        for pop in range(pops)
        for site in range(sites)
    ]
    return lax.ppermute(array, ("pop", "site"), pairs)


def flip(index):
    return index ^ 1


def stay(index):
    return index


def per_device(
    profile, panel, visit_person, visit_owner, visit_row, visit_start, visit_length, tile_loc
):
    pop_count = lax.axis_size("pop")
    visits = visit_person.shape[0]
    persons, slots = profile.shape
    width = panel.shape[1]
    capacity = visits // pop_count * 3 // 2
    rows = pop_count * capacity
    as_row = lambda x: x.reshape(1, visits)
    send, person_rows = pl.pallas_call(
        lambda *refs: pack_kernel(pop_count, *refs),
        out_shape=(
            pltpu.VMEM((rows, 128 + width), BF16),
            pltpu.VMEM((persons, rows), BF16),
        ),
        in_specs=vmem(7),
        out_specs=tuple(vmem(2)),
        name="pack",
    )(
        profile.T,
        panel,
        as_row(visit_person),
        as_row(visit_owner),
        as_row(visit_row),
        as_row(visit_start),
        as_row(visit_length),
    )
    tile_locs = [
        tile_loc,
        swap(tile_loc, flip, stay),
        swap(tile_loc, stay, flip),
        swap(tile_loc, flip, flip),
    ]
    got = exchange(send)
    smem = [pl.BlockSpec(memory_space=pltpu.SMEM)] * 4
    half = (HALF * slots, width)
    kept, given = pl.pallas_call(
        lambda *refs: moment_kernel(slots, *refs),
        out_shape=(pltpu.VMEM(half, F32), pltpu.VMEM(half, BF16)),
        in_specs=smem + vmem(1),
        out_specs=tuple(vmem(2)),
        name="moments",
    )(*tile_locs, got)
    steps = (
        (flip, stay),
        (stay, lambda site: site ^ 2),
        (stay, lambda site: (6 - site) % 8 if site % 2 == 0 else 8 - site),
    )
    for step, partners in enumerate(steps):
        far = in_vmem(swap(given, *partners))
        if step < 2:
            kept, given = pl.pallas_call(
                add_kernel,
                out_shape=(pltpu.VMEM(half, F32), pltpu.VMEM(half, BF16)),
                in_specs=vmem(2),
                out_specs=tuple(vmem(2)),
                name="add",
            )(in_vmem(kept), far)
        else:
            given = pl.pallas_call(
                last_add_kernel,
                out_shape=pltpu.VMEM(half, BF16),
                in_specs=vmem(2),
                out_specs=vmem(1)[0],
                name="last_add",
            )(in_vmem(kept), far)
    other = in_vmem(swap(given, flip, stay))
    result = pl.pallas_call(
        lambda *refs: apply_kernel(slots, *refs),
        out_shape=pltpu.VMEM((rows, width), BF16),
        in_specs=smem + vmem(3),
        out_specs=vmem(1)[0],
        scratch_shapes=[pltpu.VMEM((LOCATIONS * 128, width), BF16)],
        name="apply",
    )(*tile_locs, got, in_vmem(given), other)
    returned = exchange(result)
    return pl.pallas_call(
        finish_kernel,
        out_shape=jax.ShapeDtypeStruct((persons, width), BF16),
        in_specs=vmem(2),
        out_specs=vmem(1)[0],
        name="finish",
    )(in_vmem(person_rows), returned)


def solution(mesh):
    both = P(("pop", "site"))
    wide = P(("pop", "site"), None)
    return jax.shard_map(
        per_device,
        mesh=mesh,
        in_specs=(wide, wide, both, both, both, both, both, both),
        out_specs=wide,
        check_vma=False,
    )
```

```python
import jax
import jax.numpy as jnp
from jax import lax
from jax.experimental import pallas as pl
from jax.experimental.pallas import tpu as pltpu
from jax.sharding import PartitionSpec as P

BF16 = jnp.bfloat16
F32 = jnp.float32
LOCATIONS = 8
HALF = LOCATIONS // 2
TILES = 8
NT = (((1,), (1,)), ((), ()))


def iota(shape, axis):
    return lax.broadcasted_iota(jnp.int32, shape, axis)


def matmul(a, b):
    return jnp.dot(a, b, preferred_element_type=F32)


def matmul_nt(a, b):
    return lax.dot_general(a, b, NT, preferred_element_type=F32)


def as_bf16(mask):
    return jnp.where(mask, 1.0, 0.0).astype(BF16)


def pack_kernel(
    pop_count,
    profile_ref,
    panel_ref,
    person_ref,
    owner_ref,
    row_ref,
    start_ref,
    length_ref,
    send_ref,
    persons_ref,
):
    visits = person_ref.shape[1]
    slots, persons = profile_ref.shape
    rows = send_ref.shape[0]
    capacity = rows // pop_count
    owner = owner_ref[...]
    start = start_ref[...]
    finish = jnp.minimum(start + length_ref[...], slots)
    tile = (row_ref[...] >> 7) + TILES * (lax.axis_index("site") & 1)
    owner_hot = iota((pop_count, visits), 0) == owner
    earlier = as_bf16(iota((visits, visits), 0) < iota((visits, visits), 1))
    before = matmul(as_bf16(owner_hot), earlier)
    position = jnp.sum(jnp.where(owner_hot, before, 0.0), axis=0, keepdims=True)
    slot = owner * capacity + position.astype(jnp.int32)
    place = as_bf16(iota((rows, visits), 0) == slot)
    person_hot = as_bf16(iota((persons, visits), 0) == person_ref[...])
    line = iota((128, visits), 0)
    facts = jnp.where(line == 0, start, jnp.where(line == 1, finish, jnp.where(line == 2, tile, 0)))
    table = jnp.concatenate([person_hot, facts.astype(F32).astype(BF16)], axis=0)
    placed = matmul_nt(place, table)
    hot = placed[:, :persons].astype(BF16)
    start_at = placed[:, persons : persons + 1]
    finish_at = placed[:, persons + 1 : persons + 2]
    tile_at = placed[:, persons + 2 : persons + 3]
    no_slots = jnp.zeros((128 - slots, persons), BF16)
    weights = matmul_nt(hot, jnp.concatenate([profile_ref[...], no_slots], axis=0))
    lane = iota((rows, 128), 1)
    lane_f = lane.astype(F32)
    inside = (lane_f >= start_at) & (lane_f < finish_at)
    weights = jnp.where(inside, weights, 0.0)
    weights = jnp.where(lane == slots, tile_at, weights)
    send_ref[:, :128] = weights.astype(BF16)
    send_ref[:, 128:] = matmul(hot, panel_ref[...]).astype(BF16)
    persons_ref[...] = matmul_nt(person_hot, place).astype(BF16)


def stamp_kernel(slots, pop_count, mine_ref, sibling_ref, send_ref, out_ref):
    rows = send_ref.shape[0]
    capacity = rows // pop_count
    shape = (capacity, 128)
    core = lax.axis_index("pop") & 1
    lane = iota(shape, 1)
    inside = (lane >= slots + TILES) & (lane < slots + 2 * TILES)
    first = jnp.where(core == 0, mine_ref[...], sibling_ref[...]).astype(F32)
    second = jnp.where(core == 0, sibling_ref[...], mine_ref[...]).astype(F32)
    for owner in range(pop_count):
        part = pl.ds(owner * capacity, capacity)
        stamp = jnp.broadcast_to(second if owner % 2 else first, shape)
        old = send_ref[part, :128].astype(F32)
        out_ref[part, :128] = jnp.where(inside, stamp, old).astype(BF16)
    out_ref[:, 128:] = send_ref[:, 128:]


def masked_moments(weights, place, panel, locations):
    masked = [jnp.where(place == l, weights, 0.0).astype(BF16) for l in locations]
    return matmul(jnp.concatenate(masked, axis=0), panel)


def give_kernel(slots, pop_count, got_ref, give_ref, flipped_ref, place_ref):
    rows = got_ref.shape[0]
    unit = as_bf16(iota((128, 128), 0) == iota((128, 128), 1))
    flipped = matmul_nt(unit, got_ref[:, :128])
    tile = flipped[slots : slots + 1, :]
    table = flipped[slots + TILES : slots + 2 * TILES, :]
    capacity = rows // pop_count
    pop = lax.axis_index("pop")
    start = (pop - (pop & 1)) * capacity
    column = iota((TILES, rows), 1)
    even = jnp.sum(jnp.where(column == start, table, 0.0), axis=1, keepdims=True)
    odd = jnp.sum(jnp.where(column == start + capacity, table, 0.0), axis=1, keepdims=True)
    line = iota((TILES, rows), 0).astype(F32)
    chosen = jnp.where(tile == line, even, jnp.where(tile == line + TILES, odd, 0.0))
    place = jnp.sum(chosen, axis=0, keepdims=True).astype(jnp.int32) ^ (HALF * (pop & 1))
    weights = flipped[:slots, :]
    panel = got_ref[:, 128:]
    give_ref[...] = masked_moments(weights, place, panel, range(HALF, LOCATIONS)).astype(BF16)
    flipped_ref[...] = weights.astype(BF16)
    place_ref[...] = jnp.broadcast_to(place, place_ref.shape).astype(F32)


def keep_kernel(flipped_ref, place_ref, got_ref, keep_ref):
    weights = flipped_ref[...].astype(F32)
    place = place_ref[0:1, :].astype(jnp.int32)
    keep_ref[...] = masked_moments(weights, place, got_ref[:, 128:], range(HALF))


def columns_kernel(slots, place_ref, columns_ref):
    place = jnp.transpose(place_ref[...])[:, 0:1]
    inside = iota(columns_ref.shape, 1) < slots
    columns_ref[...] = jnp.where(inside, place, -1.0).astype(BF16)


def add_kernel(own_ref, far_ref, sum_ref, give_ref):
    total = own_ref[...] + far_ref[...].astype(F32)
    sum_ref[...] = total
    give_ref[...] = total.astype(BF16)


def last_add_kernel(own_ref, far_ref, give_ref):
    give_ref[...] = (own_ref[...] + far_ref[...].astype(F32)).astype(BF16)


def widen(slots, half_ref, wide_ref):
    for l in range(HALF):
        wide_ref[pl.ds(l * 128, slots), :] = half_ref[pl.ds(l * slots, slots), :]
        wide_ref[pl.ds(l * 128 + slots, 128 - slots), :] = jnp.zeros((128 - slots, 128), BF16)


def masked_weights(columns_ref, got_ref, location):
    weights = got_ref[:, :128].astype(F32)
    return jnp.where(columns_ref[...].astype(F32) == location, weights, 0.0).astype(BF16)


def own_kernel(slots, columns_ref, got_ref, own_ref, part_ref, spread_ref, wide_ref):
    widen(slots, own_ref, wide_ref)
    spread = [masked_weights(columns_ref, got_ref, l) for l in range(HALF)]
    part_ref[...] = matmul(jnp.concatenate(spread, axis=1), wide_ref[...])
    for l in range(HALF):
        spread_ref[:, l * 128 : (l + 1) * 128] = masked_weights(columns_ref, got_ref, HALF + l)


def other_kernel(slots, spread_ref, other_ref, part_ref, result_ref, wide_ref):
    widen(slots, other_ref, wide_ref)
    result = part_ref[...] + matmul(spread_ref[...], wide_ref[...])
    result_ref[...] = (result * (1.0 / slots)).astype(BF16)


def finish_kernel(persons_ref, results_ref, out_ref):
    out_ref[...] = matmul(persons_ref[...], results_ref[...]).astype(BF16)


def vmem(count):
    return [pl.BlockSpec(memory_space=pltpu.VMEM)] * count


def call(kernel, name, outs, *args, scratch=(), cost=0.5):
    return pl.pallas_call(
        kernel,
        out_shape=tuple(pltpu.VMEM(shape, kind) for shape, kind in outs),
        in_specs=vmem(len(args)),
        out_specs=tuple(vmem(len(outs))),
        scratch_shapes=list(scratch),
        cost_estimate=pl.CostEstimate(
            flops=int(cost * 5e8), bytes_accessed=int(cost * 2e6), transcendentals=0
        ),
        name=name,
    )(*args)


def in_vmem(array):
    return pltpu.with_memory_space_constraint(array, pltpu.VMEM)


def exchange(array):
    pops, sites = lax.axis_size("pop"), lax.axis_size("site")
    groups = [
        [(pop * 2 + core) * sites + pair * 2 + odd for pop in range(pops // 2) for odd in range(2)]
        for core in range(2)
        for pair in range(sites // 2)
    ]
    blocks = array.reshape((pops, -1, array.shape[-1]))
    moved = lax.all_to_all(
        blocks, ("pop", "site"), 0, 0, tiled=True, axis_index_groups=groups
    )
    return in_vmem(moved.reshape(array.shape))


def swap(array, pop_partner, site_partner):
    pops, sites = lax.axis_size("pop"), lax.axis_size("site")
    pairs = [
        (pop * sites + site, pop_partner(pop) * sites + site_partner(site))
        for pop in range(pops)
        for site in range(sites)
    ]
    return lax.ppermute(array, ("pop", "site"), pairs)


def flip(index):
    return index ^ 1


def stay(index):
    return index


def per_device(
    profile, panel, visit_person, visit_owner, visit_row, visit_start, visit_length, tile_loc
):
    pop_count = lax.axis_size("pop")
    visits = visit_person.shape[0]
    persons, slots = profile.shape
    width = panel.shape[1]
    capacity = visits // pop_count * 3 // 2
    rows = pop_count * capacity
    as_row = lambda x: x.reshape(1, visits)
    place_row = lambda x: jnp.pad(x, (slots + TILES, 128 - slots - 2 * TILES)).reshape(1, 128)
    mine = place_row(tile_loc)
    sibling = in_vmem(swap(mine, flip, stay))
    send, person_rows = call(
        lambda *refs: pack_kernel(pop_count, *refs),
        "pack",
        [((rows, 128 + width), BF16), ((persons, rows), BF16)],
        profile.T,
        panel,
        as_row(visit_person),
        as_row(visit_owner),
        as_row(visit_row),
        as_row(visit_start),
        as_row(visit_length),
    )
    (send,) = call(
        lambda *refs: stamp_kernel(slots, pop_count, *refs),
        "stamp",
        [((rows, 128 + width), BF16)],
        in_vmem(mine),
        sibling,
        in_vmem(send),
    )
    got = exchange(send)
    half = (HALF * slots, width)
    give, flipped, place = call(
        lambda *refs: give_kernel(slots, pop_count, *refs),
        "give",
        [(half, BF16), ((slots, rows), BF16), ((8, rows), F32)],
        got,
    )
    flipped, place = in_vmem(flipped), in_vmem(place)
    far = in_vmem(swap(give, flip, stay))
    (keep,) = call(keep_kernel, "keep", [(half, F32)], flipped, place, got, cost=0.6)
    keep, give = call(add_kernel, "add", [(half, F32), (half, BF16)], in_vmem(keep), far)
    moved = swap(give, stay, lambda site: site ^ 2)
    (columns,) = call(
        lambda *refs: columns_kernel(slots, *refs), "columns", [((rows, 128), BF16)], place
    )
    moved, columns = lax.optimization_barrier((moved, columns))
    far, columns = in_vmem(moved), in_vmem(columns)
    keep, give = call(add_kernel, "add", [(half, F32), (half, BF16)], in_vmem(keep), far)
    far = in_vmem(
        swap(give, stay, lambda site: (6 - site) % 8 if site % 2 == 0 else 8 - site)
    )
    (give,) = call(last_add_kernel, "last_add", [(half, BF16)], in_vmem(keep), far)
    other = in_vmem(swap(give, flip, stay))
    wide = [pltpu.VMEM((HALF * 128, width), BF16)]
    part, spread = call(
        lambda *refs: own_kernel(slots, *refs),
        "own",
        [((rows, width), F32), ((rows, HALF * 128), BF16)],
        columns,
        got,
        in_vmem(give),
        scratch=wide,
        cost=0.6,
    )
    (result,) = call(
        lambda *refs: other_kernel(slots, *refs),
        "other",
        [((rows, width), BF16)],
        in_vmem(spread),
        other,
        in_vmem(part),
        scratch=wide,
    )
    returned = exchange(result)
    return pl.pallas_call(
        finish_kernel,
        out_shape=jax.ShapeDtypeStruct((persons, width), BF16),
        in_specs=vmem(2),
        out_specs=vmem(1)[0],
        name="finish",
    )(in_vmem(person_rows), returned)


def solution(mesh):
    both = P(("pop", "site"))
    wide = P(("pop", "site"), None)
    return jax.shard_map(
        per_device,
        mesh=mesh,
        in_specs=(wide, wide, both, both, both, both, both, both),
        out_specs=wide,
        check_vma=False,
    )
```

```python
import jax
import jax.numpy as jnp
from jax import lax
from jax.experimental import pallas as pl
from jax.experimental.pallas import tpu as pltpu
from jax.sharding import PartitionSpec as P

BF16 = jnp.bfloat16
F32 = jnp.float32
LOCATIONS = 8
HALF = LOCATIONS // 2
TILES = 8
NT = (((1,), (1,)), ((), ()))


def iota(shape, axis):
    return lax.broadcasted_iota(jnp.int32, shape, axis)


def matmul(a, b):
    return jnp.dot(a, b, preferred_element_type=F32)


def matmul_nt(a, b):
    return lax.dot_general(a, b, NT, preferred_element_type=F32)


def as_bf16(mask):
    return jnp.where(mask, 1.0, 0.0).astype(BF16)


def pack_kernel(
    pop_count,
    profile_ref,
    panel_ref,
    person_ref,
    owner_ref,
    row_ref,
    start_ref,
    length_ref,
    send_ref,
    persons_ref,
):
    visits = person_ref.shape[1]
    slots, persons = profile_ref.shape
    rows = send_ref.shape[0]
    capacity = rows // pop_count
    owner = owner_ref[...]
    start = start_ref[...]
    finish = jnp.minimum(start + length_ref[...], slots)
    tile = (row_ref[...] >> 7) + TILES * (lax.axis_index("site") & 1)
    owner_hot = iota((pop_count, visits), 0) == owner
    marks = jnp.where(owner_hot, 1.0, 0.0)
    earlier = as_bf16(iota((128, 128), 0) < iota((128, 128), 1))
    chunks = [marks[:, at : at + 128] for at in range(0, visits, 128)]
    counts = matmul(jnp.concatenate(chunks, axis=0).astype(BF16), earlier)
    seen = jnp.zeros((pop_count, 1), F32)
    positions = []
    for number, chunk in enumerate(chunks):
        before = counts[number * pop_count : (number + 1) * pop_count] + seen
        positions.append(jnp.sum(chunk * before, axis=0, keepdims=True))
        seen = seen + jnp.sum(chunk, axis=1, keepdims=True)
    position = jnp.concatenate(positions, axis=1)
    slot = owner * capacity + position.astype(jnp.int32)
    place = as_bf16(iota((rows, visits), 0) == slot)
    person_hot = as_bf16(iota((persons, visits), 0) == person_ref[...])
    line = iota((128, visits), 0)
    facts = jnp.where(line == 0, start, jnp.where(line == 1, finish, jnp.where(line == 2, tile, 0)))
    table = jnp.concatenate([person_hot, facts.astype(F32).astype(BF16)], axis=0)
    placed = matmul_nt(place, table)
    hot = placed[:, :persons].astype(BF16)
    start_at = placed[:, persons : persons + 1]
    finish_at = placed[:, persons + 1 : persons + 2]
    tile_at = placed[:, persons + 2 : persons + 3]
    no_slots = jnp.zeros((128 - slots, persons), BF16)
    weights = matmul_nt(hot, jnp.concatenate([profile_ref[...], no_slots], axis=0))
    lane = iota((rows, 128), 1)
    lane_f = lane.astype(F32)
    inside = (lane_f >= start_at) & (lane_f < finish_at)
    weights = jnp.where(inside, weights, 0.0)
    weights = jnp.where(lane == slots, tile_at, weights)
    send_ref[:, :128] = weights.astype(BF16)
    send_ref[:, 128:] = matmul(hot, panel_ref[...]).astype(BF16)
    persons_ref[...] = hot


def stamp_kernel(slots, pop_count, mine_ref, sibling_ref, send_ref, out_ref):
    rows = send_ref.shape[0]
    capacity = rows // pop_count
    shape = (capacity, 128)
    core = lax.axis_index("pop") & 1
    lane = iota(shape, 1)
    inside = (lane >= slots + TILES) & (lane < slots + 2 * TILES)
    mine, sibling = mine_ref[...].astype(F32), sibling_ref[...].astype(F32)
    pair = (TILES, TILES)
    mine, sibling = jnp.broadcast_to(mine, pair), jnp.broadcast_to(sibling, pair)
    line, column = iota((TILES, 128), 0), iota((TILES, 128), 1)
    shift = as_bf16(column == line + slots + TILES)
    first = matmul(jnp.where(core == 0, mine, sibling).astype(BF16), shift)[0:1, :]
    second = matmul(jnp.where(core == 0, sibling, mine).astype(BF16), shift)[0:1, :]
    for owner in range(pop_count):
        part = pl.ds(owner * capacity, capacity)
        stamp = jnp.broadcast_to(second if owner % 2 else first, shape)
        old = send_ref[part, :128].astype(F32)
        out_ref[part, :128] = jnp.where(inside, stamp, old).astype(BF16)
    out_ref[:, 128:] = send_ref[:, 128:]


def masked_moments(weights, place, panel, locations):
    masked = [jnp.where(place == l, weights, 0.0).astype(BF16) for l in locations]
    return matmul(jnp.concatenate(masked, axis=0), panel)


def give_kernel(slots, pop_count, got_ref, give_ref, flipped_ref, place_ref):
    rows = got_ref.shape[0]
    unit = as_bf16(iota((128, 128), 0) == iota((128, 128), 1))
    flipped = matmul_nt(unit, got_ref[:, :128])
    tile = flipped[slots : slots + 1, :]
    table = flipped[slots + TILES : slots + 2 * TILES, :]
    capacity = rows // pop_count
    pop = lax.axis_index("pop")
    start = (pop - (pop & 1)) * capacity
    column = iota((TILES, rows), 1)
    even = jnp.sum(jnp.where(column == start, table, 0.0), axis=1, keepdims=True)
    odd = jnp.sum(jnp.where(column == start + capacity, table, 0.0), axis=1, keepdims=True)
    line = iota((TILES, rows), 0).astype(F32)
    chosen = jnp.where(tile == line, even, jnp.where(tile == line + TILES, odd, 0.0))
    place = jnp.sum(chosen, axis=0, keepdims=True).astype(jnp.int32) ^ (HALF * (pop & 1))
    weights = flipped[:slots, :]
    panel = got_ref[:, 128:]
    give_ref[...] = masked_moments(weights, place, panel, range(HALF, LOCATIONS)).astype(BF16)
    flipped_ref[...] = weights.astype(BF16)
    place_ref[...] = jnp.broadcast_to(place, place_ref.shape).astype(F32)


def keep_kernel(flipped_ref, place_ref, got_ref, keep_ref):
    weights = flipped_ref[...].astype(F32)
    place = place_ref[0:1, :].astype(jnp.int32)
    keep_ref[...] = masked_moments(weights, place, got_ref[:, 128:], range(HALF))


def columns_kernel(slots, place_ref, columns_ref):
    place = jnp.transpose(place_ref[...])[:, 0:1]
    inside = iota(columns_ref.shape, 1) < slots
    columns_ref[...] = jnp.where(inside, place, -1.0).astype(BF16)


def flip_kernel(rows_ref, flipped_ref):
    flipped_ref[...] = jnp.transpose(rows_ref[...].astype(F32)).astype(BF16)


def add_kernel(own_ref, far_ref, sum_ref, give_ref):
    total = own_ref[...] + far_ref[...].astype(F32)
    sum_ref[...] = total
    give_ref[...] = total.astype(BF16)


def last_add_kernel(own_ref, far_ref, give_ref):
    give_ref[...] = (own_ref[...] + far_ref[...].astype(F32)).astype(BF16)


def widen(slots, half_ref, wide_ref):
    for l in range(HALF):
        wide_ref[pl.ds(l * 128, slots), :] = half_ref[pl.ds(l * slots, slots), :]
        wide_ref[pl.ds(l * 128 + slots, 128 - slots), :] = jnp.zeros((128 - slots, 128), BF16)


def masked_weights(columns_ref, got_ref, location):
    weights = got_ref[:, :128].astype(F32)
    return jnp.where(columns_ref[...].astype(F32) == location, weights, 0.0).astype(BF16)


def own_kernel(slots, columns_ref, got_ref, own_ref, part_ref, spread_ref, wide_ref):
    widen(slots, own_ref, wide_ref)
    spread = [masked_weights(columns_ref, got_ref, l) for l in range(HALF)]
    part_ref[...] = matmul(jnp.concatenate(spread, axis=1), wide_ref[...])
    for l in range(HALF):
        spread_ref[:, l * 128 : (l + 1) * 128] = masked_weights(columns_ref, got_ref, HALF + l)


def other_kernel(slots, spread_ref, other_ref, part_ref, result_ref, wide_ref):
    widen(slots, other_ref, wide_ref)
    result = part_ref[...] + matmul(spread_ref[...], wide_ref[...])
    result_ref[...] = (result * (1.0 / slots)).astype(BF16)


def finish_kernel(persons_ref, results_ref, out_ref):
    out_ref[...] = matmul(persons_ref[...], results_ref[...]).astype(BF16)


def vmem(count):
    return [pl.BlockSpec(memory_space=pltpu.VMEM)] * count


def call(kernel, name, outs, *args, scratch=(), cost=0.5):
    return pl.pallas_call(
        kernel,
        out_shape=tuple(pltpu.VMEM(shape, kind) for shape, kind in outs),
        in_specs=vmem(len(args)),
        out_specs=tuple(vmem(len(outs))),
        scratch_shapes=list(scratch),
        cost_estimate=pl.CostEstimate(
            flops=int(cost * 5e8), bytes_accessed=int(cost * 2e6), transcendentals=0
        ),
        name=name,
    )(*args)


def in_vmem(array):
    return pltpu.with_memory_space_constraint(array, pltpu.VMEM)


def exchange(array):
    pops, sites = lax.axis_size("pop"), lax.axis_size("site")
    groups = [
        [(pop * 2 + core) * sites + pair * 2 + odd for pop in range(pops // 2) for odd in range(2)]
        for core in range(2)
        for pair in range(sites // 2)
    ]
    blocks = array.reshape((pops, -1, array.shape[-1]))
    moved = lax.all_to_all(
        blocks, ("pop", "site"), 0, 0, tiled=True, axis_index_groups=groups
    )
    return in_vmem(moved.reshape(array.shape))


def swap(array, pop_partner, site_partner):
    pops, sites = lax.axis_size("pop"), lax.axis_size("site")
    pairs = [
        (pop * sites + site, pop_partner(pop) * sites + site_partner(site))
        for pop in range(pops)
        for site in range(sites)
    ]
    return lax.ppermute(array, ("pop", "site"), pairs)


def flip(index):
    return index ^ 1


def stay(index):
    return index


def per_device(
    profile, panel, visit_person, visit_owner, visit_row, visit_start, visit_length, tile_loc
):
    pop_count = lax.axis_size("pop")
    visits = visit_person.shape[0]
    persons, slots = profile.shape
    width = panel.shape[1]
    capacity = visits // pop_count * 3 // 2
    rows = pop_count * capacity
    as_row = lambda x: x.reshape(1, visits)
    mine = tile_loc.reshape(1, TILES)
    sibling = in_vmem(swap(mine, flip, stay))
    send, person_rows = call(
        lambda *refs: pack_kernel(pop_count, *refs),
        "pack",
        [((rows, 128 + width), BF16), ((rows, persons), BF16)],
        profile.T,
        panel,
        as_row(visit_person),
        as_row(visit_owner),
        as_row(visit_row),
        as_row(visit_start),
        as_row(visit_length),
    )
    (send,) = call(
        lambda *refs: stamp_kernel(slots, pop_count, *refs),
        "stamp",
        [((rows, 128 + width), BF16)],
        mine,
        sibling,
        in_vmem(send),
    )
    got = exchange(send)
    half = (HALF * slots, width)
    give, flipped, place = call(
        lambda *refs: give_kernel(slots, pop_count, *refs),
        "give",
        [(half, BF16), ((slots, rows), BF16), ((8, rows), F32)],
        got,
    )
    flipped, place = in_vmem(flipped), in_vmem(place)
    far = in_vmem(swap(give, flip, stay))
    (keep,) = call(keep_kernel, "keep", [(half, F32)], flipped, place, got, cost=0.6)
    keep, give = call(add_kernel, "add", [(half, F32), (half, BF16)], in_vmem(keep), far)
    moved = swap(give, stay, lambda site: site ^ 2)
    (columns,) = call(
        lambda *refs: columns_kernel(slots, *refs), "columns", [((rows, 128), BF16)], place
    )
    moved, columns = lax.optimization_barrier((moved, columns))
    far, columns = in_vmem(moved), in_vmem(columns)
    keep, give = call(add_kernel, "add", [(half, F32), (half, BF16)], in_vmem(keep), far)
    moved = swap(give, stay, lambda site: (6 - site) % 8 if site % 2 == 0 else 8 - site)
    (person_rows,) = call(flip_kernel, "flip", [((persons, rows), BF16)], in_vmem(person_rows))
    moved, person_rows = lax.optimization_barrier((moved, person_rows))
    far = in_vmem(moved)
    (give,) = call(last_add_kernel, "last_add", [(half, BF16)], in_vmem(keep), far)
    other = in_vmem(swap(give, flip, stay))
    wide = [pltpu.VMEM((HALF * 128, width), BF16)]
    part, spread = call(
        lambda *refs: own_kernel(slots, *refs),
        "own",
        [((rows, width), F32), ((rows, HALF * 128), BF16)],
        columns,
        got,
        in_vmem(give),
        scratch=wide,
        cost=0.6,
    )
    (result,) = call(
        lambda *refs: other_kernel(slots, *refs),
        "other",
        [((rows, width), BF16)],
        in_vmem(spread),
        other,
        in_vmem(part),
        scratch=wide,
    )
    returned = exchange(result)
    return pl.pallas_call(
        finish_kernel,
        out_shape=jax.ShapeDtypeStruct((persons, width), BF16),
        in_specs=vmem(2),
        out_specs=vmem(1)[0],
        name="finish",
    )(in_vmem(person_rows), returned)


def solution(mesh):
    both = P(("pop", "site"))
    wide = P(("pop", "site"), None)
    return jax.shard_map(
        per_device,
        mesh=mesh,
        in_specs=(wide, wide, both, both, both, both, both, both),
        out_specs=wide,
        check_vma=False,
    )
```

```python
import functools

import jax
import jax.numpy as jnp
from jax import lax
from jax.experimental import pallas as pl
from jax.experimental.pallas import tpu as pltpu
from jax.sharding import PartitionSpec as P

BF16 = jnp.bfloat16
F32 = jnp.float32
LOCATIONS = 8
HALF = LOCATIONS // 2
TILES = 8
NT = (((1,), (1,)), ((), ()))


def iota(shape, axis):
    return lax.broadcasted_iota(jnp.int32, shape, axis)


def matmul(a, b):
    return jnp.dot(a, b, preferred_element_type=F32)


def matmul_nt(a, b):
    return lax.dot_general(a, b, NT, preferred_element_type=F32)


def as_bf16(mask):
    return jnp.where(mask, 1.0, 0.0).astype(BF16)


def pack_kernel(
    pop_count,
    profile_ref,
    panel_ref,
    person_ref,
    owner_ref,
    row_ref,
    start_ref,
    length_ref,
    send_ref,
    persons_ref,
):
    visits = person_ref.shape[1]
    slots, persons = profile_ref.shape
    rows = send_ref.shape[0]
    capacity = rows // pop_count
    owner = owner_ref[...]
    start = start_ref[...]
    finish = jnp.minimum(start + length_ref[...], slots)
    tile = (row_ref[...] >> 7) + TILES * (lax.axis_index("site") & 1)
    owner_hot = iota((pop_count, visits), 0) == owner
    marks = jnp.where(owner_hot, 1.0, 0.0)
    earlier = as_bf16(iota((128, 128), 0) < iota((128, 128), 1))
    chunks = [marks[:, at : at + 128] for at in range(0, visits, 128)]
    counts = matmul(jnp.concatenate(chunks, axis=0).astype(BF16), earlier)
    seen = jnp.zeros((pop_count, 1), F32)
    positions = []
    for number, chunk in enumerate(chunks):
        before = counts[number * pop_count : (number + 1) * pop_count] + seen
        positions.append(jnp.sum(chunk * before, axis=0, keepdims=True))
        seen = seen + jnp.sum(chunk, axis=1, keepdims=True)
    position = jnp.concatenate(positions, axis=1)
    slot = owner * capacity + position.astype(jnp.int32)
    place = as_bf16(iota((rows, visits), 0) == slot)
    person_hot = as_bf16(iota((persons, visits), 0) == person_ref[...])
    line = iota((128, visits), 0)
    facts = jnp.where(line == 0, start, jnp.where(line == 1, finish, jnp.where(line == 2, tile, 0)))
    table = jnp.concatenate([person_hot, facts.astype(F32).astype(BF16)], axis=0)
    placed = matmul_nt(place, table)
    hot = placed[:, :persons].astype(BF16)
    start_at = placed[:, persons : persons + 1]
    finish_at = placed[:, persons + 1 : persons + 2]
    tile_at = placed[:, persons + 2 : persons + 3]
    no_slots = jnp.zeros((128 - slots, persons), BF16)
    weights = matmul_nt(hot, jnp.concatenate([profile_ref[...], no_slots], axis=0))
    lane = iota((rows, 128), 1)
    lane_f = lane.astype(F32)
    inside = (lane_f >= start_at) & (lane_f < finish_at)
    weights = jnp.where(inside, weights, 0.0)
    weights = jnp.where(lane == slots, tile_at, weights)
    send_ref[:, :128] = weights.astype(BF16)
    send_ref[:, 128:] = matmul(hot, panel_ref[...]).astype(BF16)
    persons_ref[...] = hot


def stamp_kernel(slots, pop_count, mine_ref, sibling_ref, send_ref, out_ref):
    rows = send_ref.shape[0]
    capacity = rows // pop_count
    shape = (capacity, 128)
    core = lax.axis_index("pop") & 1
    lane = iota(shape, 1)
    inside = (lane >= slots + TILES) & (lane < slots + 2 * TILES)
    mine, sibling = mine_ref[...].astype(F32), sibling_ref[...].astype(F32)
    pair = (TILES, TILES)
    mine, sibling = jnp.broadcast_to(mine, pair), jnp.broadcast_to(sibling, pair)
    line, column = iota((TILES, 128), 0), iota((TILES, 128), 1)
    shift = as_bf16(column == line + slots + TILES)
    first = matmul(jnp.where(core == 0, mine, sibling).astype(BF16), shift)[0:1, :]
    second = matmul(jnp.where(core == 0, sibling, mine).astype(BF16), shift)[0:1, :]
    for owner in range(pop_count):
        part = pl.ds(owner * capacity, capacity)
        stamp = jnp.broadcast_to(second if owner % 2 else first, shape)
        old = send_ref[part, :128].astype(F32)
        out_ref[part, :128] = jnp.where(inside, stamp, old).astype(BF16)
    out_ref[:, 128:] = send_ref[:, 128:]


def masked_moments(weights, place, panel, locations):
    masked = [jnp.where(place == l, weights, 0.0).astype(BF16) for l in locations]
    return matmul(jnp.concatenate(masked, axis=0), panel)


def give_kernel(slots, pop_count, got_ref, give_ref, flipped_ref, place_ref):
    rows = got_ref.shape[0]
    unit = as_bf16(iota((128, 128), 0) == iota((128, 128), 1))
    flipped = matmul_nt(unit, got_ref[:, :128])
    tile = flipped[slots : slots + 1, :]
    table = flipped[slots + TILES : slots + 2 * TILES, :]
    capacity = rows // pop_count
    pop = lax.axis_index("pop")
    start = (pop - (pop & 1)) * capacity
    column = iota((TILES, rows), 1)
    even = jnp.sum(jnp.where(column == start, table, 0.0), axis=1, keepdims=True)
    odd = jnp.sum(jnp.where(column == start + capacity, table, 0.0), axis=1, keepdims=True)
    line = iota((TILES, rows), 0).astype(F32)
    chosen = jnp.where(tile == line, even, jnp.where(tile == line + TILES, odd, 0.0))
    place = jnp.sum(chosen, axis=0, keepdims=True).astype(jnp.int32) ^ (HALF * (pop & 1))
    weights = flipped[:slots, :]
    panel = got_ref[:, 128:]
    give_ref[...] = masked_moments(weights, place, panel, range(HALF, LOCATIONS)).astype(BF16)
    flipped_ref[...] = weights.astype(BF16)
    place_ref[...] = jnp.broadcast_to(place, place_ref.shape).astype(F32)


def keep_kernel(flipped_ref, place_ref, got_ref, keep_ref):
    weights = flipped_ref[...].astype(F32)
    place = place_ref[0:1, :].astype(jnp.int32)
    keep_ref[...] = masked_moments(weights, place, got_ref[:, 128:], range(HALF))


def columns_kernel(slots, place_ref, columns_ref):
    place = jnp.transpose(place_ref[...])[:, 0:1]
    inside = iota(columns_ref.shape, 1) < slots
    columns_ref[...] = jnp.where(inside, place, -1.0).astype(BF16)


def flip_kernel(rows_ref, flipped_ref):
    flipped_ref[...] = jnp.transpose(rows_ref[...].astype(F32)).astype(BF16)


def add_kernel(own_ref, far_ref, sum_ref, give_ref):
    total = own_ref[...] + far_ref[...].astype(F32)
    sum_ref[...] = total
    give_ref[...] = total.astype(BF16)


def last_add_kernel(own_ref, far_ref, give_ref):
    give_ref[...] = (own_ref[...] + far_ref[...].astype(F32)).astype(BF16)


def widen(slots, half_ref, wide_ref):
    for l in range(HALF):
        wide_ref[pl.ds(l * 128, slots), :] = half_ref[pl.ds(l * slots, slots), :]
        wide_ref[pl.ds(l * 128 + slots, 128 - slots), :] = jnp.zeros((128 - slots, 128), BF16)


def masked_weights(columns_ref, got_ref, location):
    weights = got_ref[:, :128].astype(F32)
    return jnp.where(columns_ref[...].astype(F32) == location, weights, 0.0).astype(BF16)


def own_kernel(slots, columns_ref, got_ref, own_ref, part_ref, spread_ref, wide_ref):
    widen(slots, own_ref, wide_ref)
    spread = [masked_weights(columns_ref, got_ref, l) for l in range(HALF)]
    part_ref[...] = matmul(jnp.concatenate(spread, axis=1), wide_ref[...])
    for l in range(HALF):
        spread_ref[:, l * 128 : (l + 1) * 128] = masked_weights(columns_ref, got_ref, HALF + l)


def other_kernel(slots, spread_ref, other_ref, part_ref, result_ref, wide_ref):
    widen(slots, other_ref, wide_ref)
    result = part_ref[...] + matmul(spread_ref[...], wide_ref[...])
    result_ref[...] = (result * (1.0 / slots)).astype(BF16)


def finish_kernel(persons_ref, results_ref, out_ref):
    out_ref[...] = matmul(persons_ref[...], results_ref[...]).astype(BF16)


def vmem(count):
    return [pl.BlockSpec(memory_space=pltpu.VMEM)] * count


def call(kernel, name, outs, *args, scratch=(), cost=0.5):
    return pl.pallas_call(
        kernel,
        out_shape=tuple(pltpu.VMEM(shape, kind) for shape, kind in outs),
        in_specs=vmem(len(args)),
        out_specs=tuple(vmem(len(outs))),
        scratch_shapes=list(scratch),
        cost_estimate=pl.CostEstimate(
            flops=int(cost * 5e8), bytes_accessed=int(cost * 2e6), transcendentals=0
        ),
        name=name,
    )(*args)


def in_vmem(array):
    return pltpu.with_memory_space_constraint(array, pltpu.VMEM)


def exchange(array):
    pops, sites = lax.axis_size("pop"), lax.axis_size("site")
    groups = [
        [(pop * 2 + core) * sites + pair * 2 + odd for pop in range(pops // 2) for odd in range(2)]
        for core in range(2)
        for pair in range(sites // 2)
    ]
    blocks = array.reshape((pops, -1, array.shape[-1]))
    moved = lax.all_to_all(
        blocks, ("pop", "site"), 0, 0, tiled=True, axis_index_groups=groups
    )
    return in_vmem(moved.reshape(array.shape))


def swap(array, partner):
    pops, sites = lax.axis_size("pop"), lax.axis_size("site")
    pairs = []
    for pop in range(pops):
        for site in range(sites):
            far_pop, far_site = partner(pop, site)
            pairs.append((pop * sites + site, far_pop * sites + far_site))
    return lax.ppermute(array, ("pop", "site"), pairs)


def sibling_core(pop, site):
    return pop ^ 1, site


def site_step(step, pop, site):
    if (step + pop) % 2 == 0:
        return pop, site ^ 2
    return pop, (8 - site if site % 2 else 6 - site) % 8


def per_device(
    profile, panel, visit_person, visit_owner, visit_row, visit_start, visit_length, tile_loc
):
    pop_count = lax.axis_size("pop")
    visits = visit_person.shape[0]
    persons, slots = profile.shape
    width = panel.shape[1]
    capacity = visits // pop_count * 3 // 2
    rows = pop_count * capacity
    as_row = lambda x: x.reshape(1, visits)
    mine = tile_loc.reshape(1, TILES)
    sibling = in_vmem(swap(mine, sibling_core))
    send, person_rows = call(
        lambda *refs: pack_kernel(pop_count, *refs),
        "pack",
        [((rows, 128 + width), BF16), ((rows, persons), BF16)],
        profile.T,
        panel,
        as_row(visit_person),
        as_row(visit_owner),
        as_row(visit_row),
        as_row(visit_start),
        as_row(visit_length),
    )
    (send,) = call(
        lambda *refs: stamp_kernel(slots, pop_count, *refs),
        "stamp",
        [((rows, 128 + width), BF16)],
        in_vmem(mine),
        sibling,
        in_vmem(send),
    )
    got = exchange(send)
    half = (HALF * slots, width)
    give, flipped, place = call(
        lambda *refs: give_kernel(slots, pop_count, *refs),
        "give",
        [(half, BF16), ((slots, rows), BF16), ((8, rows), F32)],
        got,
    )
    flipped, place = in_vmem(flipped), in_vmem(place)
    far = in_vmem(swap(give, sibling_core))
    (keep,) = call(keep_kernel, "keep", [(half, F32)], flipped, place, got, cost=0.6)
    keep, give = call(add_kernel, "add", [(half, F32), (half, BF16)], in_vmem(keep), far)
    moved = swap(give, functools.partial(site_step, 0))
    (columns,) = call(
        lambda *refs: columns_kernel(slots, *refs), "columns", [((rows, 128), BF16)], place
    )
    moved, columns = lax.optimization_barrier((moved, columns))
    far, columns = in_vmem(moved), in_vmem(columns)
    keep, give = call(add_kernel, "add", [(half, F32), (half, BF16)], in_vmem(keep), far)
    moved = swap(give, functools.partial(site_step, 1))
    (person_rows,) = call(flip_kernel, "flip", [((persons, rows), BF16)], in_vmem(person_rows))
    moved, person_rows = lax.optimization_barrier((moved, person_rows))
    far = in_vmem(moved)
    (give,) = call(last_add_kernel, "last_add", [(half, BF16)], in_vmem(keep), far)
    other = in_vmem(swap(give, sibling_core))
    wide = [pltpu.VMEM((HALF * 128, width), BF16)]
    part, spread = call(
        lambda *refs: own_kernel(slots, *refs),
        "own",
        [((rows, width), F32), ((rows, HALF * 128), BF16)],
        columns,
        got,
        in_vmem(give),
        scratch=wide,
        cost=0.6,
    )
    (result,) = call(
        lambda *refs: other_kernel(slots, *refs),
        "other",
        [((rows, width), BF16)],
        in_vmem(spread),
        other,
        in_vmem(part),
        scratch=wide,
    )
    returned = exchange(result)
    return pl.pallas_call(
        finish_kernel,
        out_shape=jax.ShapeDtypeStruct((persons, width), BF16),
        in_specs=vmem(2),
        out_specs=vmem(1)[0],
        name="finish",
    )(in_vmem(person_rows), returned)


def solution(mesh):
    both = P(("pop", "site"))
    wide = P(("pop", "site"), None)
    return jax.shard_map(
        per_device,
        mesh=mesh,
        in_specs=(wide, wide, both, both, both, both, both, both),
        out_specs=wide,
        check_vma=False,
    )
```

```python
import functools

import jax
import jax.numpy as jnp
from jax import lax
from jax.experimental import pallas as pl
from jax.experimental.pallas import tpu as pltpu
from jax.sharding import PartitionSpec as P

BF16 = jnp.bfloat16
F32 = jnp.float32
LOCATIONS = 8
HALF = LOCATIONS // 2
TILES = 8
NT = (((1,), (1,)), ((), ()))


def iota(shape, axis):
    return lax.broadcasted_iota(jnp.int32, shape, axis)


def matmul(a, b):
    return jnp.dot(a, b, preferred_element_type=F32)


def matmul_nt(a, b):
    return lax.dot_general(a, b, NT, preferred_element_type=F32)


def as_bf16(mask):
    return jnp.where(mask, 1.0, 0.0).astype(BF16)


def pack_kernel(
    pop_count,
    profile_ref,
    panel_ref,
    person_ref,
    owner_ref,
    row_ref,
    start_ref,
    length_ref,
    send_ref,
    persons_ref,
):
    visits = person_ref.shape[1]
    slots, persons = profile_ref.shape
    rows = send_ref.shape[0]
    capacity = rows // pop_count
    owner = owner_ref[...]
    start = start_ref[...]
    finish = jnp.minimum(start + length_ref[...], slots)
    tile = (row_ref[...] >> 7) + TILES * (lax.axis_index("site") & 1)
    owner_hot = iota((pop_count, visits), 0) == owner
    marks = jnp.where(owner_hot, 1.0, 0.0)
    earlier = as_bf16(iota((128, 128), 0) < iota((128, 128), 1))
    chunks = [marks[:, at : at + 128] for at in range(0, visits, 128)]
    counts = matmul(jnp.concatenate(chunks, axis=0).astype(BF16), earlier)
    seen = jnp.zeros((pop_count, 1), F32)
    positions = []
    for number, chunk in enumerate(chunks):
        before = counts[number * pop_count : (number + 1) * pop_count] + seen
        positions.append(jnp.sum(chunk * before, axis=0, keepdims=True))
        seen = seen + jnp.sum(chunk, axis=1, keepdims=True)
    position = jnp.concatenate(positions, axis=1)
    slot = owner * capacity + position.astype(jnp.int32)
    place = as_bf16(iota((rows, visits), 0) == slot)
    person_hot = as_bf16(iota((persons, visits), 0) == person_ref[...])
    line = iota((128, visits), 0)
    facts = jnp.where(line == 0, start, jnp.where(line == 1, finish, jnp.where(line == 2, tile, 0)))
    table = jnp.concatenate([person_hot, facts.astype(F32).astype(BF16)], axis=0)
    placed = matmul_nt(place, table)
    hot = placed[:, :persons].astype(BF16)
    start_at = placed[:, persons : persons + 1]
    finish_at = placed[:, persons + 1 : persons + 2]
    tile_at = placed[:, persons + 2 : persons + 3]
    no_slots = jnp.zeros((128 - slots, persons), BF16)
    weights = matmul_nt(hot, jnp.concatenate([profile_ref[...], no_slots], axis=0))
    lane = iota((rows, 128), 1)
    lane_f = lane.astype(F32)
    inside = (lane_f >= start_at) & (lane_f < finish_at)
    weights = jnp.where(inside, weights, 0.0)
    weights = jnp.where(lane == slots, tile_at, weights)
    send_ref[:, :128] = weights.astype(BF16)
    send_ref[:, 128:] = matmul(hot, panel_ref[...]).astype(BF16)
    persons_ref[...] = hot


def as_column(row):
    size = row.shape[1]
    square = jnp.broadcast_to(row.astype(F32), (size, size))
    diagonal = iota((size, size), 0) == iota((size, size), 1)
    return jnp.sum(jnp.where(diagonal, square, 0.0), axis=1, keepdims=True)


def masked_moments(weights, place, panel, locations):
    masked = [jnp.where(place == l, weights, 0.0).astype(BF16) for l in locations]
    return matmul(jnp.concatenate(masked, axis=0), panel)


def give_kernel(slots, *refs):
    mine, sibling, neighbour, diagonal = [ref[...] for ref in refs[:4]]
    got_ref, give_ref, flipped_ref, place_ref = refs[4:]
    rows = got_ref.shape[0]
    core = lax.axis_index("pop") & 1
    parity = lax.axis_index("site") & 1
    near = jnp.where(core == parity, mine, sibling)
    far = jnp.where(core == parity, neighbour, diagonal)
    even = as_column(jnp.where(parity == 0, near, far))
    odd = as_column(jnp.where(parity == 0, far, near))
    unit = as_bf16(iota((128, 128), 0) == iota((128, 128), 1))
    flipped = matmul_nt(unit, got_ref[:, :128])
    tile = flipped[slots : slots + 1, :]
    line = iota((TILES, rows), 0).astype(F32)
    chosen = jnp.where(tile == line, even, jnp.where(tile == line + TILES, odd, 0.0))
    place = jnp.sum(chosen, axis=0, keepdims=True).astype(jnp.int32) ^ (HALF * core)
    weights = flipped[:slots, :]
    panel = got_ref[:, 128:]
    give_ref[...] = masked_moments(weights, place, panel, range(HALF, LOCATIONS)).astype(BF16)
    flipped_ref[...] = weights.astype(BF16)
    place_ref[...] = jnp.broadcast_to(place, place_ref.shape).astype(F32)


def keep_kernel(flipped_ref, place_ref, got_ref, keep_ref):
    weights = flipped_ref[...].astype(F32)
    place = place_ref[0:1, :].astype(jnp.int32)
    keep_ref[...] = masked_moments(weights, place, got_ref[:, 128:], range(HALF))


def columns_kernel(slots, place_ref, columns_ref):
    place = jnp.transpose(place_ref[...])[:, 0:1]
    inside = iota(columns_ref.shape, 1) < slots
    columns_ref[...] = jnp.where(inside, place, -1.0).astype(BF16)


def flip_kernel(rows_ref, flipped_ref):
    flipped_ref[...] = jnp.transpose(rows_ref[...].astype(F32)).astype(BF16)


def add_kernel(own_ref, far_ref, sum_ref, give_ref):
    total = own_ref[...] + far_ref[...].astype(F32)
    sum_ref[...] = total
    give_ref[...] = total.astype(BF16)


def last_add_kernel(own_ref, far_ref, give_ref):
    give_ref[...] = (own_ref[...] + far_ref[...].astype(F32)).astype(BF16)


def widen(slots, half_ref, wide_ref):
    for l in range(HALF):
        wide_ref[pl.ds(l * 128, slots), :] = half_ref[pl.ds(l * slots, slots), :]
        wide_ref[pl.ds(l * 128 + slots, 128 - slots), :] = jnp.zeros((128 - slots, 128), BF16)


def masked_weights(columns_ref, got_ref, location):
    weights = got_ref[:, :128].astype(F32)
    return jnp.where(columns_ref[...].astype(F32) == location, weights, 0.0).astype(BF16)


def own_kernel(slots, columns_ref, got_ref, own_ref, part_ref, spread_ref, wide_ref):
    widen(slots, own_ref, wide_ref)
    spread = [masked_weights(columns_ref, got_ref, l) for l in range(HALF)]
    part_ref[...] = matmul(jnp.concatenate(spread, axis=1), wide_ref[...])
    for l in range(HALF):
        spread_ref[:, l * 128 : (l + 1) * 128] = masked_weights(columns_ref, got_ref, HALF + l)


def other_kernel(slots, spread_ref, other_ref, part_ref, result_ref, wide_ref):
    widen(slots, other_ref, wide_ref)
    result = part_ref[...] + matmul(spread_ref[...], wide_ref[...])
    result_ref[...] = (result * (1.0 / slots)).astype(BF16)


def finish_kernel(persons_ref, results_ref, out_ref):
    out_ref[...] = matmul(persons_ref[...], results_ref[...]).astype(BF16)


def vmem(count):
    return [pl.BlockSpec(memory_space=pltpu.VMEM)] * count


def call(kernel, name, outs, *args, scratch=(), cost=0.5):
    return pl.pallas_call(
        kernel,
        out_shape=tuple(pltpu.VMEM(shape, kind) for shape, kind in outs),
        in_specs=vmem(len(args)),
        out_specs=tuple(vmem(len(outs))),
        scratch_shapes=list(scratch),
        cost_estimate=pl.CostEstimate(
            flops=int(cost * 5e8), bytes_accessed=int(cost * 2e6), transcendentals=0
        ),
        name=name,
    )(*args)


def in_vmem(array):
    return pltpu.with_memory_space_constraint(array, pltpu.VMEM)


def exchange(array):
    pops, sites = lax.axis_size("pop"), lax.axis_size("site")
    groups = [
        [(pop * 2 + core) * sites + pair * 2 + odd for pop in range(pops // 2) for odd in range(2)]
        for core in range(2)
        for pair in range(sites // 2)
    ]
    blocks = array.reshape((pops, -1, array.shape[-1]))
    moved = lax.all_to_all(
        blocks, ("pop", "site"), 0, 0, tiled=True, axis_index_groups=groups
    )
    return in_vmem(moved.reshape(array.shape))


def swap(array, partner):
    pops, sites = lax.axis_size("pop"), lax.axis_size("site")
    pairs = []
    for pop in range(pops):
        for site in range(sites):
            far_pop, far_site = partner(pop, site)
            pairs.append((pop * sites + site, far_pop * sites + far_site))
    return lax.ppermute(array, ("pop", "site"), pairs)


def sibling_core(pop, site):
    return pop ^ 1, site


def site_step(step, pop, site):
    if (step + pop) % 2 == 0:
        return pop, site ^ 2
    return pop, (8 - site if site % 2 else 6 - site) % 8


def per_device(
    profile, panel, visit_person, visit_owner, visit_row, visit_start, visit_length, tile_loc
):
    pop_count = lax.axis_size("pop")
    visits = visit_person.shape[0]
    persons, slots = profile.shape
    width = panel.shape[1]
    capacity = visits // pop_count * 3 // 2
    rows = pop_count * capacity
    as_row = lambda x: x.reshape(1, visits)
    send, person_rows = call(
        lambda *refs: pack_kernel(pop_count, *refs),
        "pack",
        [((rows, 128 + width), BF16), ((rows, persons), BF16)],
        profile.T,
        panel,
        as_row(visit_person),
        as_row(visit_owner),
        as_row(visit_row),
        as_row(visit_start),
        as_row(visit_length),
    )
    mine = tile_loc.reshape(1, TILES)
    neighbour_site = lambda pop, site: (pop, site ^ 1)
    diagonal = lambda pop, site: (pop ^ 1, site ^ 1)
    tables = [mine] + [swap(mine, far) for far in (sibling_core, neighbour_site, diagonal)]
    got = exchange(send)
    half = (HALF * slots, width)
    give, flipped, place = call(
        lambda *refs: give_kernel(slots, *refs),
        "give",
        [(half, BF16), ((slots, rows), BF16), ((8, rows), F32)],
        *[in_vmem(table) for table in tables],
        got,
    )
    flipped, place = in_vmem(flipped), in_vmem(place)
    far = in_vmem(swap(give, sibling_core))
    (keep,) = call(keep_kernel, "keep", [(half, F32)], flipped, place, got, cost=0.6)
    keep, give = call(add_kernel, "add", [(half, F32), (half, BF16)], in_vmem(keep), far)
    moved = swap(give, functools.partial(site_step, 0))
    (columns,) = call(
        lambda *refs: columns_kernel(slots, *refs), "columns", [((rows, 128), BF16)], place
    )
    moved, columns = lax.optimization_barrier((moved, columns))
    far, columns = in_vmem(moved), in_vmem(columns)
    keep, give = call(add_kernel, "add", [(half, F32), (half, BF16)], in_vmem(keep), far)
    moved = swap(give, functools.partial(site_step, 1))
    (person_rows,) = call(flip_kernel, "flip", [((persons, rows), BF16)], in_vmem(person_rows))
    moved, person_rows = lax.optimization_barrier((moved, person_rows))
    far = in_vmem(moved)
    (give,) = call(last_add_kernel, "last_add", [(half, BF16)], in_vmem(keep), far)
    other = in_vmem(swap(give, sibling_core))
    wide = [pltpu.VMEM((HALF * 128, width), BF16)]
    part, spread = call(
        lambda *refs: own_kernel(slots, *refs),
        "own",
        [((rows, width), F32), ((rows, HALF * 128), BF16)],
        columns,
        got,
        in_vmem(give),
        scratch=wide,
        cost=0.6,
    )
    (result,) = call(
        lambda *refs: other_kernel(slots, *refs),
        "other",
        [((rows, width), BF16)],
        in_vmem(spread),
        other,
        in_vmem(part),
        scratch=wide,
    )
    returned = exchange(result)
    return pl.pallas_call(
        finish_kernel,
        out_shape=jax.ShapeDtypeStruct((persons, width), BF16),
        in_specs=vmem(2),
        out_specs=vmem(1)[0],
        name="finish",
    )(in_vmem(person_rows), returned)


def solution(mesh):
    both = P(("pop", "site"))
    wide = P(("pop", "site"), None)
    return jax.shard_map(
        per_device,
        mesh=mesh,
        in_specs=(wide, wide, both, both, both, both, both, both),
        out_specs=wide,
        check_vma=False,
    )
```

```python
import functools

import jax
import jax.numpy as jnp
from jax import lax
from jax.experimental import pallas as pl
from jax.experimental.pallas import tpu as pltpu
from jax.sharding import PartitionSpec as P

BF16 = jnp.bfloat16
F32 = jnp.float32
LOCATIONS = 8
HALF = LOCATIONS // 2
TILES = 8
NT = (((1,), (1,)), ((), ()))


def iota(shape, axis):
    return lax.broadcasted_iota(jnp.int32, shape, axis)


def matmul(a, b):
    return jnp.dot(a, b, preferred_element_type=F32)


def matmul_nt(a, b):
    return lax.dot_general(a, b, NT, preferred_element_type=F32)


def as_bf16(mask):
    return jnp.where(mask, 1.0, 0.0).astype(BF16)


def pack_kernel(
    pop_count,
    profile_ref,
    panel_ref,
    person_ref,
    owner_ref,
    row_ref,
    start_ref,
    length_ref,
    tile_loc_ref,
    send_ref,
    persons_ref,
    table_ref,
):
    visits = person_ref.shape[1]
    slots, persons = profile_ref.shape
    rows = send_ref.shape[0]
    capacity = rows // pop_count
    owner = owner_ref[...]
    start = start_ref[...]
    finish = jnp.minimum(start + length_ref[...], slots)
    tile = (row_ref[...] >> 7) + TILES * (lax.axis_index("site") & 1)
    owner_hot = iota((pop_count, visits), 0) == owner
    marks = jnp.where(owner_hot, 1.0, 0.0)
    earlier = as_bf16(iota((128, 128), 0) < iota((128, 128), 1))
    chunks = [marks[:, at : at + 128] for at in range(0, visits, 128)]
    counts = matmul(jnp.concatenate(chunks, axis=0).astype(BF16), earlier)
    seen = jnp.zeros((pop_count, 1), F32)
    positions = []
    for number, chunk in enumerate(chunks):
        before = counts[number * pop_count : (number + 1) * pop_count] + seen
        positions.append(jnp.sum(chunk * before, axis=0, keepdims=True))
        seen = seen + jnp.sum(chunk, axis=1, keepdims=True)
    position = jnp.concatenate(positions, axis=1)
    slot = owner * capacity + position.astype(jnp.int32)
    place = as_bf16(iota((rows, visits), 0) == slot)
    person_hot = as_bf16(iota((persons, visits), 0) == person_ref[...])
    line = iota((128, visits), 0)
    facts = jnp.where(line == 0, start, jnp.where(line == 1, finish, jnp.where(line == 2, tile, 0)))
    table = jnp.concatenate([person_hot, facts.astype(F32).astype(BF16)], axis=0)
    placed = matmul_nt(place, table)
    hot = placed[:, :persons].astype(BF16)
    start_at = placed[:, persons : persons + 1]
    finish_at = placed[:, persons + 1 : persons + 2]
    tile_at = placed[:, persons + 2 : persons + 3]
    no_slots = jnp.zeros((128 - slots, persons), BF16)
    weights = matmul_nt(hot, jnp.concatenate([profile_ref[...], no_slots], axis=0))
    lane = iota((rows, 128), 1)
    lane_f = lane.astype(F32)
    inside = (lane_f >= start_at) & (lane_f < finish_at)
    weights = jnp.where(inside, weights, 0.0)
    weights = jnp.where(lane == slots, tile_at, weights)
    send_ref[:, :128] = weights.astype(BF16)
    send_ref[:, 128:] = matmul(hot, panel_ref[...]).astype(BF16)
    persons_ref[...] = hot
    table_ref[...] = tile_loc_ref[...]


def as_column(row):
    size = row.shape[1]
    square = jnp.broadcast_to(row.astype(F32), (size, size))
    diagonal = iota((size, size), 0) == iota((size, size), 1)
    return jnp.sum(jnp.where(diagonal, square, 0.0), axis=1, keepdims=True)


def masked_moments(weights, place, panel, locations):
    masked = [jnp.where(place == l, weights, 0.0).astype(BF16) for l in locations]
    return matmul(jnp.concatenate(masked, axis=0), panel)


def give_kernel(slots, *refs):
    mine, sibling, neighbour, diagonal = [ref[...] for ref in refs[:4]]
    got_ref, give_ref, flipped_ref, place_ref = refs[4:]
    rows = got_ref.shape[0]
    core = lax.axis_index("pop") & 1
    parity = lax.axis_index("site") & 1
    near = jnp.where(core == parity, mine, sibling)
    far = jnp.where(core == parity, neighbour, diagonal)
    even = as_column(jnp.where(parity == 0, near, far))
    odd = as_column(jnp.where(parity == 0, far, near))
    unit = as_bf16(iota((128, 128), 0) == iota((128, 128), 1))
    flipped = matmul_nt(unit, got_ref[:, :128])
    tile = flipped[slots : slots + 1, :]
    line = iota((TILES, rows), 0).astype(F32)
    chosen = jnp.where(tile == line, even, jnp.where(tile == line + TILES, odd, 0.0))
    place = jnp.sum(chosen, axis=0, keepdims=True).astype(jnp.int32) ^ (HALF * core)
    weights = flipped[:slots, :]
    panel = got_ref[:, 128:]
    give_ref[...] = masked_moments(weights, place, panel, range(HALF, LOCATIONS)).astype(BF16)
    flipped_ref[...] = weights.astype(BF16)
    place_ref[...] = jnp.broadcast_to(place, place_ref.shape).astype(F32)


def keep_kernel(flipped_ref, place_ref, got_ref, keep_ref):
    weights = flipped_ref[...].astype(F32)
    place = place_ref[0:1, :].astype(jnp.int32)
    keep_ref[...] = masked_moments(weights, place, got_ref[:, 128:], range(HALF))


def columns_kernel(slots, place_ref, columns_ref):
    place = jnp.transpose(place_ref[...])[:, 0:1]
    inside = iota(columns_ref.shape, 1) < slots
    columns_ref[...] = jnp.where(inside, place, -1.0).astype(BF16)


def flip_kernel(rows_ref, flipped_ref):
    flipped_ref[...] = jnp.transpose(rows_ref[...].astype(F32)).astype(BF16)


def add_kernel(own_ref, far_ref, sum_ref, give_ref):
    total = own_ref[...] + far_ref[...].astype(F32)
    sum_ref[...] = total
    give_ref[...] = total.astype(BF16)


def last_add_kernel(own_ref, far_ref, give_ref):
    give_ref[...] = (own_ref[...] + far_ref[...].astype(F32)).astype(BF16)


def widen(slots, half_ref, wide_ref):
    for l in range(HALF):
        wide_ref[pl.ds(l * 128, slots), :] = half_ref[pl.ds(l * slots, slots), :]
        wide_ref[pl.ds(l * 128 + slots, 128 - slots), :] = jnp.zeros((128 - slots, 128), BF16)


def masked_weights(columns_ref, got_ref, location):
    weights = got_ref[:, :128].astype(F32)
    return jnp.where(columns_ref[...].astype(F32) == location, weights, 0.0).astype(BF16)


def own_kernel(slots, columns_ref, got_ref, own_ref, part_ref, spread_ref, wide_ref):
    widen(slots, own_ref, wide_ref)
    spread = [masked_weights(columns_ref, got_ref, l) for l in range(HALF)]
    part_ref[...] = matmul(jnp.concatenate(spread, axis=1), wide_ref[...])
    for l in range(HALF):
        spread_ref[:, l * 128 : (l + 1) * 128] = masked_weights(columns_ref, got_ref, HALF + l)


def other_kernel(slots, spread_ref, other_ref, part_ref, result_ref, wide_ref):
    widen(slots, other_ref, wide_ref)
    result = part_ref[...] + matmul(spread_ref[...], wide_ref[...])
    result_ref[...] = (result * (1.0 / slots)).astype(BF16)


def finish_kernel(persons_ref, results_ref, out_ref):
    out_ref[...] = matmul(persons_ref[...], results_ref[...]).astype(BF16)


def vmem(count):
    return [pl.BlockSpec(memory_space=pltpu.VMEM)] * count


def call(kernel, name, outs, *args, scratch=(), cost=0.5):
    return pl.pallas_call(
        kernel,
        out_shape=tuple(pltpu.VMEM(shape, kind) for shape, kind in outs),
        in_specs=vmem(len(args)),
        out_specs=tuple(vmem(len(outs))),
        scratch_shapes=list(scratch),
        cost_estimate=pl.CostEstimate(
            flops=int(cost * 5e8), bytes_accessed=int(cost * 2e6), transcendentals=0
        ),
        name=name,
    )(*args)


def in_vmem(array):
    return pltpu.with_memory_space_constraint(array, pltpu.VMEM)


def exchange(array):
    pops, sites = lax.axis_size("pop"), lax.axis_size("site")
    groups = [
        [(pop * 2 + core) * sites + pair * 2 + odd for pop in range(pops // 2) for odd in range(2)]
        for core in range(2)
        for pair in range(sites // 2)
    ]
    blocks = array.reshape((pops, -1, array.shape[-1]))
    moved = lax.all_to_all(
        blocks, ("pop", "site"), 0, 0, tiled=True, axis_index_groups=groups
    )
    return in_vmem(moved.reshape(array.shape))


def swap(array, partner):
    pops, sites = lax.axis_size("pop"), lax.axis_size("site")
    pairs = []
    for pop in range(pops):
        for site in range(sites):
            far_pop, far_site = partner(pop, site)
            pairs.append((pop * sites + site, far_pop * sites + far_site))
    return lax.ppermute(array, ("pop", "site"), pairs)


def sibling_core(pop, site):
    return pop ^ 1, site


def site_step(step, pop, site):
    if (step + pop) % 2 == 0:
        return pop, site ^ 2
    return pop, (8 - site if site % 2 else 6 - site) % 8


def per_device(
    profile, panel, visit_person, visit_owner, visit_row, visit_start, visit_length, tile_loc
):
    pop_count = lax.axis_size("pop")
    visits = visit_person.shape[0]
    persons, slots = profile.shape
    width = panel.shape[1]
    capacity = visits // pop_count * 3 // 2
    rows = pop_count * capacity
    as_row = lambda x: x.reshape(1, visits)
    send, person_rows, mine = call(
        lambda *refs: pack_kernel(pop_count, *refs),
        "pack",
        [((rows, 128 + width), BF16), ((rows, persons), BF16), ((1, TILES), jnp.int32)],
        profile.T,
        panel,
        as_row(visit_person),
        as_row(visit_owner),
        as_row(visit_row),
        as_row(visit_start),
        as_row(visit_length),
        tile_loc.reshape(1, TILES),
    )
    neighbour_site = lambda pop, site: (pop, site ^ 1)
    diagonal = lambda pop, site: (pop ^ 1, site ^ 1)
    tables = [mine] + [swap(mine, far) for far in (sibling_core, neighbour_site, diagonal)]
    got = exchange(send)
    half = (HALF * slots, width)
    give, flipped, place = call(
        lambda *refs: give_kernel(slots, *refs),
        "give",
        [(half, BF16), ((slots, rows), BF16), ((8, rows), F32)],
        *[in_vmem(table) for table in tables],
        got,
    )
    flipped, place = in_vmem(flipped), in_vmem(place)
    far = in_vmem(swap(give, sibling_core))
    (keep,) = call(keep_kernel, "keep", [(half, F32)], flipped, place, got, cost=0.6)
    keep, give = call(add_kernel, "add", [(half, F32), (half, BF16)], in_vmem(keep), far)
    moved = swap(give, functools.partial(site_step, 0))
    (columns,) = call(
        lambda *refs: columns_kernel(slots, *refs), "columns", [((rows, 128), BF16)], place
    )
    moved, columns = lax.optimization_barrier((moved, columns))
    far, columns = in_vmem(moved), in_vmem(columns)
    keep, give = call(add_kernel, "add", [(half, F32), (half, BF16)], in_vmem(keep), far)
    moved = swap(give, functools.partial(site_step, 1))
    (person_rows,) = call(flip_kernel, "flip", [((persons, rows), BF16)], in_vmem(person_rows))
    moved, person_rows = lax.optimization_barrier((moved, person_rows))
    far = in_vmem(moved)
    (give,) = call(last_add_kernel, "last_add", [(half, BF16)], in_vmem(keep), far)
    other = in_vmem(swap(give, sibling_core))
    wide = [pltpu.VMEM((HALF * 128, width), BF16)]
    part, spread = call(
        lambda *refs: own_kernel(slots, *refs),
        "own",
        [((rows, width), F32), ((rows, HALF * 128), BF16)],
        columns,
        got,
        in_vmem(give),
        scratch=wide,
        cost=0.6,
    )
    (result,) = call(
        lambda *refs: other_kernel(slots, *refs),
        "other",
        [((rows, width), BF16)],
        in_vmem(spread),
        other,
        in_vmem(part),
        scratch=wide,
    )
    returned = exchange(result)
    return pl.pallas_call(
        finish_kernel,
        out_shape=jax.ShapeDtypeStruct((persons, width), BF16),
        in_specs=vmem(2),
        out_specs=vmem(1)[0],
        name="finish",
    )(in_vmem(person_rows), returned)


def solution(mesh):
    both = P(("pop", "site"))
    wide = P(("pop", "site"), None)
    return jax.shard_map(
        per_device,
        mesh=mesh,
        in_specs=(wide, wide, both, both, both, both, both, both),
        out_specs=wide,
        check_vma=False,
    )
```

```python
import functools

import jax
import jax.numpy as jnp
from jax import lax
from jax.experimental import pallas as pl
from jax.experimental.pallas import tpu as pltpu
from jax.sharding import PartitionSpec as P

BF16 = jnp.bfloat16
F32 = jnp.float32
LOCATIONS = 8
HALF = LOCATIONS // 2
TILES = 8
PARTS = 4
NT = (((1,), (1,)), ((), ()))


def iota(shape, axis):
    return lax.broadcasted_iota(jnp.int32, shape, axis)


def matmul(a, b):
    return jnp.dot(a, b, preferred_element_type=F32)


def matmul_nt(a, b):
    return lax.dot_general(a, b, NT, preferred_element_type=F32)


def as_bf16(mask):
    return jnp.where(mask, 1.0, 0.0).astype(BF16)


def pack_kernel(
    pop_count,
    profile_ref,
    panel_ref,
    person_ref,
    owner_ref,
    row_ref,
    start_ref,
    length_ref,
    tile_loc_ref,
    send_ref,
    persons_ref,
    table_ref,
    message_ref,
    done_sems,
):
    visits = person_ref.shape[1]
    slots, persons = profile_ref.shape
    rows = send_ref.shape[0]
    capacity = rows // pop_count
    owner = owner_ref[...]
    start = start_ref[...]
    finish = jnp.minimum(start + length_ref[...], slots)
    tile = (row_ref[...] >> 7) + TILES * (lax.axis_index("site") & 1)
    owner_hot = iota((pop_count, visits), 0) == owner
    marks = jnp.where(owner_hot, 1.0, 0.0)
    earlier = as_bf16(iota((128, 128), 0) < iota((128, 128), 1))
    chunks = [marks[:, at : at + 128] for at in range(0, visits, 128)]
    counts = matmul(jnp.concatenate(chunks, axis=0).astype(BF16), earlier)
    seen = jnp.zeros((pop_count, 1), F32)
    positions = []
    for number, chunk in enumerate(chunks):
        before = counts[number * pop_count : (number + 1) * pop_count] + seen
        positions.append(jnp.sum(chunk * before, axis=0, keepdims=True))
        seen = seen + jnp.sum(chunk, axis=1, keepdims=True)
    position = jnp.concatenate(positions, axis=1)
    slot = owner * capacity + position.astype(jnp.int32)
    person_hot = as_bf16(iota((persons, visits), 0) == person_ref[...])
    line = iota((16, visits), 0)
    facts = jnp.where(line == 0, start, jnp.where(line == 1, finish, jnp.where(line == 2, tile, 0)))
    table = jnp.concatenate([person_hot, facts.astype(F32).astype(BF16)], axis=0)
    no_slots = jnp.zeros((128 - slots, persons), BF16)
    panel = jnp.transpose(panel_ref[...].astype(F32)).astype(BF16)
    values = jnp.concatenate([profile_ref[...], no_slots, panel], axis=0)
    part = rows // PARTS
    copies = []
    for number in range(PARTS):
        here = pl.ds(number * part, part)
        place = as_bf16(iota((part, visits), 0) + number * part == slot)
        placed = matmul_nt(place, table)
        hot = placed[:, :persons].astype(BF16)
        start_at = placed[:, persons : persons + 1]
        finish_at = placed[:, persons + 1 : persons + 2]
        tile_at = placed[:, persons + 2 : persons + 3]
        chosen = matmul_nt(hot, values)
        lane = iota((part, 128), 1)
        lane_f = lane.astype(F32)
        inside = (lane_f >= start_at) & (lane_f < finish_at)
        weights = jnp.where(inside, chosen[:, :128], 0.0)
        weights = jnp.where(lane == slots, tile_at, weights)
        message_ref[here, :128] = weights.astype(BF16)
        message_ref[here, 128:] = chosen[:, 128:].astype(BF16)
        persons_ref[here, :] = hot
        copies.append(
            pltpu.make_async_copy(
                message_ref.at[here, :], send_ref.at[here, :], done_sems.at[number]
            )
        )
        copies[-1].start()
    table_ref[...] = tile_loc_ref[...]
    for copy in copies:
        copy.wait()


def as_column(row):
    size = row.shape[1]
    square = jnp.broadcast_to(row.astype(F32), (size, size))
    diagonal = iota((size, size), 0) == iota((size, size), 1)
    return jnp.sum(jnp.where(diagonal, square, 0.0), axis=1, keepdims=True)


def masked_moments(weights, place, panel, locations):
    masked = [jnp.where(place == l, weights, 0.0).astype(BF16) for l in locations]
    return matmul(jnp.concatenate(masked, axis=0), panel)


def give_kernel(slots, *refs):
    mine, sibling, neighbour, diagonal = [ref[...] for ref in refs[:4]]
    got_ref, give_ref, flipped_ref, place_ref = refs[4:]
    rows = got_ref.shape[0]
    core = lax.axis_index("pop") & 1
    parity = lax.axis_index("site") & 1
    near = jnp.where(core == parity, mine, sibling)
    far = jnp.where(core == parity, neighbour, diagonal)
    even = as_column(jnp.where(parity == 0, near, far))
    odd = as_column(jnp.where(parity == 0, far, near))
    unit = as_bf16(iota((128, 128), 0) == iota((128, 128), 1))
    flipped = matmul_nt(unit, got_ref[:, :128])
    tile = flipped[slots : slots + 1, :]
    line = iota((TILES, rows), 0).astype(F32)
    chosen = jnp.where(tile == line, even, jnp.where(tile == line + TILES, odd, 0.0))
    place = jnp.sum(chosen, axis=0, keepdims=True).astype(jnp.int32) ^ (HALF * core)
    weights = flipped[:slots, :]
    panel = got_ref[:, 128:]
    give_ref[...] = masked_moments(weights, place, panel, range(HALF, LOCATIONS)).astype(BF16)
    flipped_ref[...] = weights.astype(BF16)
    place_ref[...] = jnp.broadcast_to(place, place_ref.shape).astype(F32)


def keep_kernel(flipped_ref, place_ref, got_ref, keep_ref):
    weights = flipped_ref[...].astype(F32)
    place = place_ref[0:1, :].astype(jnp.int32)
    keep_ref[...] = masked_moments(weights, place, got_ref[:, 128:], range(HALF))


def columns_kernel(slots, place_ref, columns_ref):
    place = jnp.transpose(place_ref[...])[:, 0:1]
    inside = iota(columns_ref.shape, 1) < slots
    columns_ref[...] = jnp.where(inside, place, -1.0).astype(BF16)


def flip_kernel(rows_ref, flipped_ref):
    flipped_ref[...] = jnp.transpose(rows_ref[...].astype(F32)).astype(BF16)


def add_kernel(own_ref, far_ref, sum_ref, give_ref):
    total = own_ref[...] + far_ref[...].astype(F32)
    sum_ref[...] = total
    give_ref[...] = total.astype(BF16)


def last_add_kernel(own_ref, far_ref, give_ref):
    give_ref[...] = (own_ref[...] + far_ref[...].astype(F32)).astype(BF16)


def widen(slots, half_ref, wide_ref):
    for l in range(HALF):
        wide_ref[pl.ds(l * 128, slots), :] = half_ref[pl.ds(l * slots, slots), :]
        wide_ref[pl.ds(l * 128 + slots, 128 - slots), :] = jnp.zeros((128 - slots, 128), BF16)


def masked_weights(columns_ref, got_ref, location):
    weights = got_ref[:, :128].astype(F32)
    return jnp.where(columns_ref[...].astype(F32) == location, weights, 0.0).astype(BF16)


def own_kernel(slots, columns_ref, got_ref, own_ref, part_ref, spread_ref, wide_ref):
    widen(slots, own_ref, wide_ref)
    spread = [masked_weights(columns_ref, got_ref, l) for l in range(HALF)]
    part_ref[...] = matmul(jnp.concatenate(spread, axis=1), wide_ref[...])
    for l in range(HALF):
        spread_ref[:, l * 128 : (l + 1) * 128] = masked_weights(columns_ref, got_ref, HALF + l)


def other_kernel(slots, spread_ref, other_ref, part_ref, result_ref, wide_ref):
    widen(slots, other_ref, wide_ref)
    result = part_ref[...] + matmul(spread_ref[...], wide_ref[...])
    result_ref[...] = (result * (1.0 / slots)).astype(BF16)


def finish_kernel(persons_ref, results_ref, out_ref):
    out_ref[...] = matmul(persons_ref[...], results_ref[...]).astype(BF16)


def vmem(count):
    return [pl.BlockSpec(memory_space=pltpu.VMEM)] * count


def call(kernel, name, outs, *args, scratch=(), cost=0.5):
    return pl.pallas_call(
        kernel,
        out_shape=tuple(pltpu.VMEM(shape, kind) for shape, kind in outs),
        in_specs=vmem(len(args)),
        out_specs=tuple(vmem(len(outs))),
        scratch_shapes=list(scratch),
        cost_estimate=pl.CostEstimate(
            flops=int(cost * 5e8), bytes_accessed=int(cost * 2e6), transcendentals=0
        ),
        name=name,
    )(*args)


def in_vmem(array):
    return pltpu.with_memory_space_constraint(array, pltpu.VMEM)


def exchange(array):
    pops, sites = lax.axis_size("pop"), lax.axis_size("site")
    groups = [
        [(pop * 2 + core) * sites + pair * 2 + odd for pop in range(pops // 2) for odd in range(2)]
        for core in range(2)
        for pair in range(sites // 2)
    ]
    blocks = array.reshape((pops, -1, array.shape[-1]))
    moved = lax.all_to_all(
        blocks, ("pop", "site"), 0, 0, tiled=True, axis_index_groups=groups
    )
    return in_vmem(moved.reshape(array.shape))


def swap(array, partner):
    pops, sites = lax.axis_size("pop"), lax.axis_size("site")
    pairs = []
    for pop in range(pops):
        for site in range(sites):
            far_pop, far_site = partner(pop, site)
            pairs.append((pop * sites + site, far_pop * sites + far_site))
    return lax.ppermute(array, ("pop", "site"), pairs)


def sibling_core(pop, site):
    return pop ^ 1, site


def site_step(step, pop, site):
    if (step + pop) % 2 == 0:
        return pop, site ^ 2
    return pop, (8 - site if site % 2 else 6 - site) % 8


def per_device(
    profile, panel, visit_person, visit_owner, visit_row, visit_start, visit_length, tile_loc
):
    pop_count = lax.axis_size("pop")
    visits = visit_person.shape[0]
    persons, slots = profile.shape
    width = panel.shape[1]
    capacity = visits // pop_count * 3 // 2
    rows = pop_count * capacity
    as_row = lambda x: x.reshape(1, visits)
    send, person_rows, mine = pl.pallas_call(
        lambda *refs: pack_kernel(pop_count, *refs),
        out_shape=(
            jax.ShapeDtypeStruct((rows, 128 + width), BF16),
            pltpu.VMEM((rows, persons), BF16),
            pltpu.VMEM((1, TILES), jnp.int32),
        ),
        in_specs=vmem(8),
        out_specs=(pl.BlockSpec(memory_space=pl.ANY), *vmem(2)),
        scratch_shapes=[
            pltpu.VMEM((rows, 128 + width), BF16),
            pltpu.SemaphoreType.DMA((PARTS,)),
        ],
        name="pack",
    )(
        profile.T,
        panel,
        as_row(visit_person),
        as_row(visit_owner),
        as_row(visit_row),
        as_row(visit_start),
        as_row(visit_length),
        tile_loc.reshape(1, TILES),
    )
    neighbour_site = lambda pop, site: (pop, site ^ 1)
    diagonal = lambda pop, site: (pop ^ 1, site ^ 1)
    tables = [mine] + [swap(mine, far) for far in (sibling_core, neighbour_site, diagonal)]
    got = exchange(send)
    half = (HALF * slots, width)
    give, flipped, place = call(
        lambda *refs: give_kernel(slots, *refs),
        "give",
        [(half, BF16), ((slots, rows), BF16), ((8, rows), F32)],
        *[in_vmem(table) for table in tables],
        got,
    )
    flipped, place = in_vmem(flipped), in_vmem(place)
    far = in_vmem(swap(give, sibling_core))
    (keep,) = call(keep_kernel, "keep", [(half, F32)], flipped, place, got, cost=0.6)
    keep, give = call(add_kernel, "add", [(half, F32), (half, BF16)], in_vmem(keep), far)
    moved = swap(give, functools.partial(site_step, 0))
    (columns,) = call(
        lambda *refs: columns_kernel(slots, *refs), "columns", [((rows, 128), BF16)], place
    )
    moved, columns = lax.optimization_barrier((moved, columns))
    far, columns = in_vmem(moved), in_vmem(columns)
    keep, give = call(add_kernel, "add", [(half, F32), (half, BF16)], in_vmem(keep), far)
    moved = swap(give, functools.partial(site_step, 1))
    (person_rows,) = call(flip_kernel, "flip", [((persons, rows), BF16)], in_vmem(person_rows))
    moved, person_rows = lax.optimization_barrier((moved, person_rows))
    far = in_vmem(moved)
    (give,) = call(last_add_kernel, "last_add", [(half, BF16)], in_vmem(keep), far)
    other = in_vmem(swap(give, sibling_core))
    wide = [pltpu.VMEM((HALF * 128, width), BF16)]
    part, spread = call(
        lambda *refs: own_kernel(slots, *refs),
        "own",
        [((rows, width), F32), ((rows, HALF * 128), BF16)],
        columns,
        got,
        in_vmem(give),
        scratch=wide,
        cost=0.6,
    )
    (result,) = call(
        lambda *refs: other_kernel(slots, *refs),
        "other",
        [((rows, width), BF16)],
        in_vmem(spread),
        other,
        in_vmem(part),
        scratch=wide,
    )
    returned = exchange(result)
    return pl.pallas_call(
        finish_kernel,
        out_shape=jax.ShapeDtypeStruct((persons, width), BF16),
        in_specs=vmem(2),
        out_specs=vmem(1)[0],
        name="finish",
    )(in_vmem(person_rows), returned)


def solution(mesh):
    both = P(("pop", "site"))
    wide = P(("pop", "site"), None)
    return jax.shard_map(
        per_device,
        mesh=mesh,
        in_specs=(wide, wide, both, both, both, both, both, both),
        out_specs=wide,
        check_vma=False,
    )
```

```python
import functools

import jax
import jax.numpy as jnp
from jax import lax
from jax.experimental import pallas as pl
from jax.experimental.pallas import tpu as pltpu
from jax.sharding import PartitionSpec as P

BF16 = jnp.bfloat16
F32 = jnp.float32
LOCATIONS = 8
HALF = LOCATIONS // 2
TILES = 8
NT = (((1,), (1,)), ((), ()))


def iota(shape, axis):
    return lax.broadcasted_iota(jnp.int32, shape, axis)


def matmul(a, b):
    return jnp.dot(a, b, preferred_element_type=F32)


def matmul_nt(a, b):
    return lax.dot_general(a, b, NT, preferred_element_type=F32)


def as_bf16(mask):
    return jnp.where(mask, 1.0, 0.0).astype(BF16)


def pack_kernel(
    pop_count,
    profile_ref,
    panel_ref,
    person_ref,
    owner_ref,
    row_ref,
    start_ref,
    length_ref,
    tile_loc_ref,
    send_ref,
    persons_ref,
    table_ref,
):
    visits = person_ref.shape[1]
    slots, persons = profile_ref.shape
    rows = send_ref.shape[0]
    capacity = rows // pop_count
    owner = owner_ref[...]
    start = start_ref[...]
    finish = jnp.minimum(start + length_ref[...], slots)
    tile = (row_ref[...] >> 7) + TILES * (lax.axis_index("site") & 1)
    owner_hot = iota((pop_count, visits), 0) == owner
    marks = jnp.where(owner_hot, 1.0, 0.0)
    earlier = as_bf16(iota((128, 128), 0) < iota((128, 128), 1))
    chunks = [marks[:, at : at + 128] for at in range(0, visits, 128)]
    counts = matmul(jnp.concatenate(chunks, axis=0).astype(BF16), earlier)
    seen = jnp.zeros((pop_count, 1), F32)
    positions = []
    for number, chunk in enumerate(chunks):
        before = counts[number * pop_count : (number + 1) * pop_count] + seen
        positions.append(jnp.sum(chunk * before, axis=0, keepdims=True))
        seen = seen + jnp.sum(chunk, axis=1, keepdims=True)
    position = jnp.concatenate(positions, axis=1)
    slot = owner * capacity + position.astype(jnp.int32)
    place = as_bf16(iota((rows, visits), 0) == slot)
    person_hot = as_bf16(iota((persons, visits), 0) == person_ref[...])
    line = iota((16, visits), 0)
    facts = jnp.where(line == 0, start, jnp.where(line == 1, finish, jnp.where(line == 2, tile, 0)))
    table = jnp.concatenate([person_hot, facts.astype(F32).astype(BF16)], axis=0)
    placed = matmul_nt(place, table)
    hot = placed[:, :persons].astype(BF16)
    start_at = placed[:, persons : persons + 1]
    finish_at = placed[:, persons + 1 : persons + 2]
    tile_at = placed[:, persons + 2 : persons + 3]
    no_slots = jnp.zeros((128 - slots, persons), BF16)
    panel = jnp.transpose(panel_ref[...].astype(F32)).astype(BF16)
    chosen = matmul_nt(hot, jnp.concatenate([profile_ref[...], no_slots, panel], axis=0))
    lane = iota((rows, 128), 1)
    lane_f = lane.astype(F32)
    inside = (lane_f >= start_at) & (lane_f < finish_at)
    weights = jnp.where(inside, chosen[:, :128], 0.0)
    weights = jnp.where(lane == slots, tile_at, weights)
    send_ref[:, :128] = weights.astype(BF16)
    send_ref[:, 128:] = chosen[:, 128:].astype(BF16)
    persons_ref[...] = hot
    table_ref[...] = tile_loc_ref[...]


def as_column(row):
    size = row.shape[1]
    square = jnp.broadcast_to(row.astype(F32), (size, size))
    diagonal = iota((size, size), 0) == iota((size, size), 1)
    return jnp.sum(jnp.where(diagonal, square, 0.0), axis=1, keepdims=True)


def masked_moments(weights, place, panel, locations):
    masked = [jnp.where(place == l, weights, 0.0).astype(BF16) for l in locations]
    return matmul(jnp.concatenate(masked, axis=0), panel)


def give_kernel(slots, *refs):
    mine, sibling, neighbour, diagonal = [ref[...] for ref in refs[:4]]
    got_ref, give_ref, flipped_ref, place_ref = refs[4:]
    rows = got_ref.shape[0]
    core = lax.axis_index("pop") & 1
    parity = lax.axis_index("site") & 1
    near = jnp.where(core == parity, mine, sibling)
    far = jnp.where(core == parity, neighbour, diagonal)
    even = as_column(jnp.where(parity == 0, near, far))
    odd = as_column(jnp.where(parity == 0, far, near))
    unit = as_bf16(iota((128, 128), 0) == iota((128, 128), 1))
    flipped = matmul_nt(unit, got_ref[:, :128])
    tile = flipped[slots : slots + 1, :]
    line = iota((TILES, rows), 0).astype(F32)
    chosen = jnp.where(tile == line, even, jnp.where(tile == line + TILES, odd, 0.0))
    place = jnp.sum(chosen, axis=0, keepdims=True).astype(jnp.int32) ^ (HALF * core)
    weights = flipped[:slots, :]
    panel = got_ref[:, 128:]
    give_ref[...] = masked_moments(weights, place, panel, range(HALF, LOCATIONS)).astype(BF16)
    flipped_ref[...] = weights.astype(BF16)
    place_ref[...] = jnp.broadcast_to(place, place_ref.shape).astype(F32)


def keep_kernel(flipped_ref, place_ref, got_ref, keep_ref):
    weights = flipped_ref[...].astype(F32)
    place = place_ref[0:1, :].astype(jnp.int32)
    keep_ref[...] = masked_moments(weights, place, got_ref[:, 128:], range(HALF))


def columns_kernel(slots, place_ref, columns_ref):
    place = jnp.transpose(place_ref[...])[:, 0:1]
    inside = iota(columns_ref.shape, 1) < slots
    columns_ref[...] = jnp.where(inside, place, -1.0).astype(BF16)


def flip_kernel(rows_ref, flipped_ref):
    flipped_ref[...] = jnp.transpose(rows_ref[...].astype(F32)).astype(BF16)


def add_kernel(own_ref, far_ref, sum_ref, give_ref):
    total = own_ref[...] + far_ref[...].astype(F32)
    sum_ref[...] = total
    give_ref[...] = total.astype(BF16)


def last_add_kernel(own_ref, far_ref, give_ref):
    give_ref[...] = (own_ref[...] + far_ref[...].astype(F32)).astype(BF16)


def widen(slots, half_ref, wide_ref):
    for l in range(HALF):
        wide_ref[pl.ds(l * 128, slots), :] = half_ref[pl.ds(l * slots, slots), :]
        wide_ref[pl.ds(l * 128 + slots, 128 - slots), :] = jnp.zeros((128 - slots, 128), BF16)


def masked_weights(columns_ref, got_ref, location):
    weights = got_ref[:, :128].astype(F32)
    return jnp.where(columns_ref[...].astype(F32) == location, weights, 0.0).astype(BF16)


def own_kernel(slots, columns_ref, got_ref, own_ref, part_ref, spread_ref, wide_ref):
    widen(slots, own_ref, wide_ref)
    spread = [masked_weights(columns_ref, got_ref, l) for l in range(HALF)]
    part_ref[...] = matmul(jnp.concatenate(spread, axis=1), wide_ref[...])
    for l in range(HALF):
        spread_ref[:, l * 128 : (l + 1) * 128] = masked_weights(columns_ref, got_ref, HALF + l)


def other_kernel(slots, spread_ref, other_ref, part_ref, result_ref, wide_ref):
    widen(slots, other_ref, wide_ref)
    result = part_ref[...] + matmul(spread_ref[...], wide_ref[...])
    result_ref[...] = (result * (1.0 / slots)).astype(BF16)


def finish_kernel(persons_ref, results_ref, out_ref):
    out_ref[...] = matmul(persons_ref[...], results_ref[...]).astype(BF16)


def vmem(count):
    return [pl.BlockSpec(memory_space=pltpu.VMEM)] * count


def call(kernel, name, outs, *args, scratch=(), cost=0.5):
    return pl.pallas_call(
        kernel,
        out_shape=tuple(pltpu.VMEM(shape, kind) for shape, kind in outs),
        in_specs=vmem(len(args)),
        out_specs=tuple(vmem(len(outs))),
        scratch_shapes=list(scratch),
        cost_estimate=pl.CostEstimate(
            flops=int(cost * 5e8), bytes_accessed=int(cost * 2e6), transcendentals=0
        ),
        name=name,
    )(*args)


def in_vmem(array):
    return pltpu.with_memory_space_constraint(array, pltpu.VMEM)


def exchange(array):
    pops, sites = lax.axis_size("pop"), lax.axis_size("site")
    groups = [
        [(pop * 2 + core) * sites + pair * 2 + odd for pop in range(pops // 2) for odd in range(2)]
        for core in range(2)
        for pair in range(sites // 2)
    ]
    blocks = array.reshape((pops, -1, array.shape[-1]))
    moved = lax.all_to_all(
        blocks, ("pop", "site"), 0, 0, tiled=True, axis_index_groups=groups
    )
    return in_vmem(moved.reshape(array.shape))


def swap(array, partner):
    pops, sites = lax.axis_size("pop"), lax.axis_size("site")
    pairs = []
    for pop in range(pops):
        for site in range(sites):
            far_pop, far_site = partner(pop, site)
            pairs.append((pop * sites + site, far_pop * sites + far_site))
    return lax.ppermute(array, ("pop", "site"), pairs)


def sibling_core(pop, site):
    return pop ^ 1, site


def site_step(step, pop, site):
    if (step + pop) % 2 == 1:
        return pop, site ^ 2
    return pop, (8 - site if site % 2 else 6 - site) % 8


def per_device(
    profile, panel, visit_person, visit_owner, visit_row, visit_start, visit_length, tile_loc
):
    pop_count = lax.axis_size("pop")
    visits = visit_person.shape[0]
    persons, slots = profile.shape
    width = panel.shape[1]
    capacity = visits // pop_count * 3 // 2
    rows = pop_count * capacity
    as_row = lambda x: x.reshape(1, visits)
    send, person_rows, mine = call(
        lambda *refs: pack_kernel(pop_count, *refs),
        "pack",
        [((rows, 128 + width), BF16), ((rows, persons), BF16), ((1, TILES), jnp.int32)],
        profile.T,
        panel,
        as_row(visit_person),
        as_row(visit_owner),
        as_row(visit_row),
        as_row(visit_start),
        as_row(visit_length),
        tile_loc.reshape(1, TILES),
    )
    neighbour_site = lambda pop, site: (pop, site ^ 1)
    diagonal = lambda pop, site: (pop ^ 1, site ^ 1)
    tables = [mine] + [swap(mine, far) for far in (sibling_core, neighbour_site, diagonal)]
    got = exchange(send)
    half = (HALF * slots, width)
    give, flipped, place = call(
        lambda *refs: give_kernel(slots, *refs),
        "give",
        [(half, BF16), ((slots, rows), BF16), ((8, rows), F32)],
        *[in_vmem(table) for table in tables],
        got,
    )
    flipped, place = in_vmem(flipped), in_vmem(place)
    far = in_vmem(swap(give, sibling_core))
    (keep,) = call(keep_kernel, "keep", [(half, F32)], flipped, place, got, cost=0.6)
    keep, give = call(add_kernel, "add", [(half, F32), (half, BF16)], in_vmem(keep), far)
    moved = swap(give, functools.partial(site_step, 0))
    (columns,) = call(
        lambda *refs: columns_kernel(slots, *refs), "columns", [((rows, 128), BF16)], place
    )
    moved, columns = lax.optimization_barrier((moved, columns))
    far, columns = in_vmem(moved), in_vmem(columns)
    keep, give = call(add_kernel, "add", [(half, F32), (half, BF16)], in_vmem(keep), far)
    moved = swap(give, functools.partial(site_step, 1))
    (person_rows,) = call(flip_kernel, "flip", [((persons, rows), BF16)], in_vmem(person_rows))
    moved, person_rows = lax.optimization_barrier((moved, person_rows))
    far = in_vmem(moved)
    (give,) = call(last_add_kernel, "last_add", [(half, BF16)], in_vmem(keep), far)
    other = in_vmem(swap(give, sibling_core))
    wide = [pltpu.VMEM((HALF * 128, width), BF16)]
    part, spread = call(
        lambda *refs: own_kernel(slots, *refs),
        "own",
        [((rows, width), F32), ((rows, HALF * 128), BF16)],
        columns,
        got,
        in_vmem(give),
        scratch=wide,
        cost=0.6,
    )
    (result,) = call(
        lambda *refs: other_kernel(slots, *refs),
        "other",
        [((rows, width), BF16)],
        in_vmem(spread),
        other,
        in_vmem(part),
        scratch=wide,
    )
    returned = exchange(result)
    return pl.pallas_call(
        finish_kernel,
        out_shape=jax.ShapeDtypeStruct((persons, width), BF16),
        in_specs=vmem(2),
        out_specs=vmem(1)[0],
        name="finish",
    )(in_vmem(person_rows), returned)


def solution(mesh):
    both = P(("pop", "site"))
    wide = P(("pop", "site"), None)
    return jax.shard_map(
        per_device,
        mesh=mesh,
        in_specs=(wide, wide, both, both, both, both, both, both),
        out_specs=wide,
        check_vma=False,
    )
```

```python
import functools

import jax
import jax.numpy as jnp
from jax import lax
from jax.experimental import pallas as pl
from jax.experimental.pallas import tpu as pltpu
from jax.sharding import PartitionSpec as P

BF16 = jnp.bfloat16
F32 = jnp.float32
LOCATIONS = 8
HALF = LOCATIONS // 2
TILES = 8
NT = (((1,), (1,)), ((), ()))


def iota(shape, axis):
    return lax.broadcasted_iota(jnp.int32, shape, axis)


def matmul(a, b):
    return jnp.dot(a, b, preferred_element_type=F32)


def matmul_nt(a, b):
    return lax.dot_general(a, b, NT, preferred_element_type=F32)


def as_bf16(mask):
    return jnp.where(mask, 1.0, 0.0).astype(BF16)


def pack_kernel(
    pop_count,
    profile_ref,
    panel_ref,
    person_ref,
    owner_ref,
    row_ref,
    start_ref,
    length_ref,
    tile_loc_ref,
    send_ref,
    persons_ref,
    table_ref,
):
    visits = person_ref.shape[1]
    slots, persons = profile_ref.shape
    rows = send_ref.shape[0]
    capacity = rows // pop_count
    owner = owner_ref[...]
    start = start_ref[...]
    finish = jnp.minimum(start + length_ref[...], slots)
    tile = (row_ref[...] >> 7) + TILES * (lax.axis_index("site") & 1)
    owner_hot = iota((pop_count, visits), 0) == owner
    marks = jnp.where(owner_hot, 1.0, 0.0)
    earlier = as_bf16(iota((128, 128), 0) < iota((128, 128), 1))
    chunks = [marks[:, at : at + 128] for at in range(0, visits, 128)]
    counts = matmul(jnp.concatenate(chunks, axis=0).astype(BF16), earlier)
    seen = jnp.zeros((pop_count, 1), F32)
    positions = []
    for number, chunk in enumerate(chunks):
        before = counts[number * pop_count : (number + 1) * pop_count] + seen
        positions.append(jnp.sum(chunk * before, axis=0, keepdims=True))
        seen = seen + jnp.sum(chunk, axis=1, keepdims=True)
    position = jnp.concatenate(positions, axis=1)
    slot = owner * capacity + position.astype(jnp.int32)
    place = as_bf16(iota((rows, visits), 0) == slot)
    person_hot = as_bf16(iota((persons, visits), 0) == person_ref[...])
    line = iota((16, visits), 0)
    facts = jnp.where(line == 0, start, jnp.where(line == 1, finish, jnp.where(line == 2, tile, 0)))
    table = jnp.concatenate([person_hot, facts.astype(F32).astype(BF16)], axis=0)
    placed = matmul_nt(place, table)
    hot = placed[:, :persons].astype(BF16)
    start_at = placed[:, persons : persons + 1]
    finish_at = placed[:, persons + 1 : persons + 2]
    tile_at = placed[:, persons + 2 : persons + 3]
    no_slots = jnp.zeros((128 - slots, persons), BF16)
    panel = jnp.transpose(panel_ref[...].astype(F32)).astype(BF16)
    chosen = matmul_nt(hot, jnp.concatenate([profile_ref[...], no_slots, panel], axis=0))
    lane = iota((rows, 128), 1)
    lane_f = lane.astype(F32)
    inside = (lane_f >= start_at) & (lane_f < finish_at)
    weights = jnp.where(inside, chosen[:, :128], 0.0)
    weights = jnp.where(lane == slots, tile_at, weights)
    send_ref[:, :128] = weights.astype(BF16)
    send_ref[:, 128:] = chosen[:, 128:].astype(BF16)
    persons_ref[...] = hot
    table_ref[...] = tile_loc_ref[...]


def as_column(row):
    size = row.shape[1]
    square = jnp.broadcast_to(row.astype(F32), (size, size))
    diagonal = iota((size, size), 0) == iota((size, size), 1)
    return jnp.sum(jnp.where(diagonal, square, 0.0), axis=1, keepdims=True)


def masked_moments(weights, place, panel, locations):
    masked = [jnp.where(place == l, weights, 0.0).astype(BF16) for l in locations]
    return matmul(jnp.concatenate(masked, axis=0), panel)


def give_kernel(slots, *refs):
    mine, sibling, neighbour, diagonal = [ref[...] for ref in refs[:4]]
    got_ref, give_ref, flipped_ref, place_ref = refs[4:]
    rows = got_ref.shape[0]
    core = lax.axis_index("pop") & 1
    parity = lax.axis_index("site") & 1
    near = jnp.where(core == parity, mine, sibling)
    far = jnp.where(core == parity, neighbour, diagonal)
    even = as_column(jnp.where(parity == 0, near, far))
    odd = as_column(jnp.where(parity == 0, far, near))
    unit = as_bf16(iota((128, 128), 0) == iota((128, 128), 1))
    flipped = matmul_nt(unit, got_ref[:, :128])
    tile = flipped[slots : slots + 1, :]
    line = iota((TILES, rows), 0).astype(F32)
    chosen = jnp.where(tile == line, even, jnp.where(tile == line + TILES, odd, 0.0))
    place = jnp.sum(chosen, axis=0, keepdims=True).astype(jnp.int32) ^ (HALF * core)
    weights = flipped[:slots, :]
    panel = got_ref[:, 128:]
    give_ref[...] = masked_moments(weights, place, panel, range(HALF, LOCATIONS)).astype(BF16)
    flipped_ref[...] = weights.astype(BF16)
    place_ref[...] = jnp.broadcast_to(place, place_ref.shape).astype(F32)


def keep_kernel(flipped_ref, place_ref, got_ref, keep_ref):
    weights = flipped_ref[...].astype(F32)
    place = place_ref[0:1, :].astype(jnp.int32)
    keep_ref[...] = masked_moments(weights, place, got_ref[:, 128:], range(HALF))


def columns_kernel(slots, place_ref, columns_ref):
    place = jnp.transpose(place_ref[...])[:, 0:1]
    inside = iota(columns_ref.shape, 1) < slots
    columns_ref[...] = jnp.where(inside, place, -1.0).astype(BF16)


def flip_kernel(rows_ref, flipped_ref):
    flipped_ref[...] = jnp.transpose(rows_ref[...].astype(F32)).astype(BF16)


def add_kernel(own_ref, far_ref, sum_ref, give_ref):
    total = own_ref[...] + far_ref[...].astype(F32)
    sum_ref[...] = total
    give_ref[...] = total.astype(BF16)


def last_add_kernel(own_ref, far_ref, give_ref):
    give_ref[...] = (own_ref[...] + far_ref[...].astype(F32)).astype(BF16)


def widen(slots, half_ref, wide_ref):
    for l in range(HALF):
        wide_ref[pl.ds(l * 128, slots), :] = half_ref[pl.ds(l * slots, slots), :]
        wide_ref[pl.ds(l * 128 + slots, 128 - slots), :] = jnp.zeros((128 - slots, 128), BF16)


def masked_weights(columns_ref, got_ref, location):
    weights = got_ref[:, :128].astype(F32)
    return jnp.where(columns_ref[...].astype(F32) == location, weights, 0.0).astype(BF16)


def own_kernel(slots, columns_ref, got_ref, own_ref, part_ref, spread_ref, wide_ref):
    widen(slots, own_ref, wide_ref)
    spread = [masked_weights(columns_ref, got_ref, l) for l in range(HALF)]
    part_ref[...] = matmul(jnp.concatenate(spread, axis=1), wide_ref[...])
    for l in range(HALF):
        spread_ref[:, l * 128 : (l + 1) * 128] = masked_weights(columns_ref, got_ref, HALF + l)


def other_kernel(slots, spread_ref, other_ref, part_ref, result_ref, wide_ref):
    widen(slots, other_ref, wide_ref)
    result = part_ref[...] + matmul(spread_ref[...], wide_ref[...])
    result_ref[...] = (result * (1.0 / slots)).astype(BF16)


def finish_kernel(persons_ref, results_ref, out_ref):
    out_ref[...] = matmul(persons_ref[...], results_ref[...]).astype(BF16)


def vmem(count):
    return [pl.BlockSpec(memory_space=pltpu.VMEM)] * count


def call(kernel, name, outs, *args, scratch=(), cost=0.5):
    return pl.pallas_call(
        kernel,
        out_shape=tuple(pltpu.VMEM(shape, kind) for shape, kind in outs),
        in_specs=vmem(len(args)),
        out_specs=tuple(vmem(len(outs))),
        scratch_shapes=list(scratch),
        cost_estimate=pl.CostEstimate(
            flops=int(cost * 5e8), bytes_accessed=int(cost * 2e6), transcendentals=0
        ),
        name=name,
    )(*args)


def in_vmem(array):
    return pltpu.with_memory_space_constraint(array, pltpu.VMEM)


def exchange(array):
    pops, sites = lax.axis_size("pop"), lax.axis_size("site")
    groups = [
        [(pop * 2 + core) * sites + pair * 2 + odd for pop in range(pops // 2) for odd in range(2)]
        for core in range(2)
        for pair in range(sites // 2)
    ]
    blocks = array.reshape((pops, -1, array.shape[-1]))
    moved = lax.all_to_all(
        blocks, ("pop", "site"), 0, 0, tiled=True, axis_index_groups=groups
    )
    return in_vmem(moved.reshape(array.shape))


def swap(array, partner):
    pops, sites = lax.axis_size("pop"), lax.axis_size("site")
    pairs = []
    for pop in range(pops):
        for site in range(sites):
            far_pop, far_site = partner(pop, site)
            pairs.append((pop * sites + site, far_pop * sites + far_site))
    return lax.ppermute(array, ("pop", "site"), pairs)


def sibling_core(pop, site):
    return pop ^ 1, site


def site_step(step, pop, site):
    if (step + pop + site) % 2 == 1:
        return pop, site ^ 2
    return pop, (8 - site if site % 2 else 6 - site) % 8


def per_device(
    profile, panel, visit_person, visit_owner, visit_row, visit_start, visit_length, tile_loc
):
    pop_count = lax.axis_size("pop")
    visits = visit_person.shape[0]
    persons, slots = profile.shape
    width = panel.shape[1]
    capacity = visits // pop_count * 3 // 2
    rows = pop_count * capacity
    as_row = lambda x: x.reshape(1, visits)
    send, person_rows, mine = call(
        lambda *refs: pack_kernel(pop_count, *refs),
        "pack",
        [((rows, 128 + width), BF16), ((rows, persons), BF16), ((1, TILES), jnp.int32)],
        profile.T,
        panel,
        as_row(visit_person),
        as_row(visit_owner),
        as_row(visit_row),
        as_row(visit_start),
        as_row(visit_length),
        tile_loc.reshape(1, TILES),
    )
    neighbour_site = lambda pop, site: (pop, site ^ 1)
    diagonal = lambda pop, site: (pop ^ 1, site ^ 1)
    tables = [mine] + [swap(mine, far) for far in (sibling_core, neighbour_site, diagonal)]
    got = exchange(send)
    half = (HALF * slots, width)
    give, flipped, place = call(
        lambda *refs: give_kernel(slots, *refs),
        "give",
        [(half, BF16), ((slots, rows), BF16), ((8, rows), F32)],
        *[in_vmem(table) for table in tables],
        got,
    )
    flipped, place = in_vmem(flipped), in_vmem(place)
    far = in_vmem(swap(give, sibling_core))
    (keep,) = call(keep_kernel, "keep", [(half, F32)], flipped, place, got, cost=0.6)
    keep, give = call(add_kernel, "add", [(half, F32), (half, BF16)], in_vmem(keep), far)
    moved = swap(give, functools.partial(site_step, 0))
    (columns,) = call(
        lambda *refs: columns_kernel(slots, *refs), "columns", [((rows, 128), BF16)], place
    )
    moved, columns = lax.optimization_barrier((moved, columns))
    far, columns = in_vmem(moved), in_vmem(columns)
    keep, give = call(add_kernel, "add", [(half, F32), (half, BF16)], in_vmem(keep), far)
    moved = swap(give, functools.partial(site_step, 1))
    (person_rows,) = call(flip_kernel, "flip", [((persons, rows), BF16)], in_vmem(person_rows))
    moved, person_rows = lax.optimization_barrier((moved, person_rows))
    far = in_vmem(moved)
    (give,) = call(last_add_kernel, "last_add", [(half, BF16)], in_vmem(keep), far)
    other = in_vmem(swap(give, sibling_core))
    wide = [pltpu.VMEM((HALF * 128, width), BF16)]
    part, spread = call(
        lambda *refs: own_kernel(slots, *refs),
        "own",
        [((rows, width), F32), ((rows, HALF * 128), BF16)],
        columns,
        got,
        in_vmem(give),
        scratch=wide,
        cost=0.6,
    )
    (result,) = call(
        lambda *refs: other_kernel(slots, *refs),
        "other",
        [((rows, width), BF16)],
        in_vmem(spread),
        other,
        in_vmem(part),
        scratch=wide,
    )
    returned = exchange(result)
    return pl.pallas_call(
        finish_kernel,
        out_shape=jax.ShapeDtypeStruct((persons, width), BF16),
        in_specs=vmem(2),
        out_specs=vmem(1)[0],
        name="finish",
    )(in_vmem(person_rows), returned)


def solution(mesh):
    both = P(("pop", "site"))
    wide = P(("pop", "site"), None)
    return jax.shard_map(
        per_device,
        mesh=mesh,
        in_specs=(wide, wide, both, both, both, both, both, both),
        out_specs=wide,
        check_vma=False,
    )
```
